32 devices in a mesh: grp: 2 (over core), swap: 16 (over z, y, x).
Axes of the slice: x: 2, y: 2, z: 4, core: 2. Of those that a mesh axis runs over, the one named last changes fastest.
Arguments:
- cells: bfloat16 [32768, 512], P(('grp', 'swap')), may hold values from -6 to 6
- counts: int32 [32768], P(('grp', 'swap')), may hold values from 64 to 512
- donor_dest: int32 [32768, 1], P(('grp', 'swap')), may hold values from 0 to 31; in each aligned block of 1024 rows (0 to 1023, 1024 to 2047, ...) at most 48 rows name the same one
- donor_tile: int32 [32768], P(('grp', 'swap')), may hold values from 0 to 2047
- depth_rank: int32 [16], replicated, may hold values from 0 to 15, as said below
- resample: bfloat16 [512, 1024], replicated, may hold values from -0.25 to 0.25
- color_gain: float32 [3], replicated, may hold values from 0.5 to 3
- color_bias: float32 [3], replicated, may hold values from -1.5 to 1.5
Outputs:
- frame: float32 [4, 1048576], P(None, ('grp', 'swap'))
The draws below stay inside these ranges and needn't reach their ends.
Inputs may be any that keep to these rules, and one draw needn't show every extreme that they name: `donor_dest`: in the rows of one device no owner is named more than 48 times, a bound that some block reaches. depth_rank[s] = s XOR m for one view mask m: the depth order is a binary partition by the bits of the brick index.
All inputs are finite; a program needn't handle non-finite values.
Results may differ from the reference program's by a relative error of at most 0.0003.
Values may be sent and summed in bfloat16 or wider, within the bound.
No kernel may reach another device: no remote copies, remote signals or barrier semaphores. Data moves between devices by JAX's collectives and lax.ppermute only.
A program may use at most 64 MiB of HBM per device.

```python
import math
import jax
import jax.numpy as jnp
import numpy as np
from jax import lax

IMG_W = 1024
IMG_H = 1024
BC = 512
TS = 1024
DEPTH = 4
NB_DEV = 1024
NB = 32768
CAP = 48
NT = 2048
N_GRP = 2
N_SWAP = 16
DEVICES = 32


def draw_depth_rank(key, part):
    view_mask = jax.random.randint(key, (), 0, N_SWAP, dtype=jnp.int32)
    return jnp.bitwise_xor(jnp.arange(N_SWAP, dtype=jnp.int32), view_mask)


def plant(values, stream_key, low, top_value):
    longest = values.shape.index(max(values.shape))
    spots = []
    for shift in (0, 1):
        where = [jax.random.randint(jax.random.fold_in(stream_key, axis), (), 0, length) for axis, length in enumerate(values.shape)]
        where[longest] = (where[longest] + shift) % values.shape[longest]
        spots.append(tuple(where))
    return values.at[spots[0]].set(low).at[spots[1]].set(top_value)


def shard_levels(own_key, dims, cuts, least, largest):
    gain = 1.0
    for dim, blocks in cuts:
        heights = jax.random.uniform(jax.random.fold_in(jax.random.fold_in(own_key, 6), dim), (blocks,), jnp.float32, least / len(cuts), largest / len(cuts))
        gain = gain * jnp.repeat(jnp.exp(heights), dims[dim] // blocks).reshape((-1,) + (1,) * (len(dims) - 1 - dim))
    return gain


def shared_out(rng, own, number, rows, number_of, top, bound, lean):
    order = jax.random.permutation(rng, number_of)
    heavy_load, ordinary = load_shares(number_of, rows * top, bound, lean, True), load_shares(number_of, rows * top, bound, lean, False)
    places = jnp.arange(number_of)

    def named(tallies, turn):
        used = int((tallies > 0).sum())
        fixed = max(1, used // 4)
        moved = fixed + (places - fixed + turn * (used - fixed)) % max(1, number_of - fixed)
        return jnp.zeros((number_of,), jnp.int32).at[order[jnp.where(places < fixed, places, moved)]].set(jnp.asarray(tallies, jnp.int32))

    tallies = jnp.where(number % 4 == 0, named(heavy_load, number // 4), named(ordinary, number - number // 4 - 1))
    mixed = jax.random.permutation(jax.random.fold_in(own, 3), number_of)
    donor, taker = mixed[0:number_of // 2 * 2:2], mixed[1:number_of // 2 * 2:2]
    slack = jnp.minimum(tallies[donor] - 1, bound - tallies[taker]) // 2
    slack = jnp.where((donor == order[0]) | (taker == order[0]) | (tallies[taker] == 0), 0, jnp.maximum(slack, 0))
    moved = jax.random.randint(jax.random.fold_in(own, 4), (number_of // 2,), 0, 1 << 20) % (slack + 1)
    tallies = tallies.at[donor].add(-moved).at[taker].add(moved)
    items = jnp.searchsorted(jnp.cumsum(tallies), jnp.arange(rows * top), side="right").astype(jnp.int32)
    table = items.reshape(top, rows).T
    table = table[jax.random.permutation(jax.random.fold_in(own, 1), rows)]
    turn = jax.random.randint(jax.random.fold_in(own, 2), (rows, 1), 0, top)
    return jnp.take_along_axis(table, (jnp.arange(top)[None, :] + turn) % top, axis=1)


def load_shares(number_of, total, limit, skew, full):
    weights = [(1 << 20) // math.isqrt(grade ** skew) + 1 for grade in range(1, number_of + 1)]
    largest = limit if full else min(limit, max(-(-total // number_of), total * weights[0] // sum(weights)))
    least = 1 if total - largest >= number_of - 1 else 0
    holding, rest = [largest] + [least] * (number_of - 1), total - largest - least * (number_of - 1)
    while rest > 0:
        free = [i for i in range(1, number_of) if holding[i] < largest] or [i for i in range(1, number_of) if holding[i] < limit]
        whole, remaining = sum([weights[i] for i in free]), rest
        for i in free:
            more = min(limit - holding[i], max(1, remaining * weights[i] // whole), rest)
            holding[i] = holding[i] + more
            rest = rest - more
    return np.array(holding)


def centred(stream_key, shape, scale, most, split=(), kind=jnp.bfloat16):
    drawn = scale * jax.random.normal(stream_key, shape, jnp.float32)
    if split:
        drawn = drawn * shard_levels(stream_key, shape, split, -0.22, 0.18)
    return jnp.clip(drawn, -most, most).astype(kind)


def setup_inputs(seed: int = 0) -> dict:
    key_list = jax.random.split(jax.random.key(seed), 9)
    cells = centred(key_list[0], (NB, BC), 1.0, 6.0, ((0, 32),))
    counts = plant(jax.random.randint(key_list[1], (NB,), BC // 8, BC + 1), jax.random.fold_in(key_list[1], 1), BC // 8, BC).astype(jnp.int32)
    donor_dest_keys = jax.random.split(jax.random.fold_in(key_list[2], 1), NB // NB_DEV)
    donor_dest_turns = jax.random.permutation(jax.random.fold_in(key_list[2], 3), NB // NB_DEV)
    donor_dest = jax.vmap(lambda own, number: shared_out(jax.random.fold_in(key_list[2], 2), own, number, NB_DEV, DEVICES, 1, CAP, 2))(donor_dest_keys, donor_dest_turns).reshape((NB, 1))
    donor_tile = plant(jax.random.randint(key_list[3], (NB,), 0, NT), jax.random.fold_in(key_list[3], 1), 0, NT - 1).astype(jnp.int32)
    depth_rank = draw_depth_rank(jax.random.fold_in(key_list[8], 71), 0)
    resample = centred(key_list[5], (BC, TS), BC ** -0.5, 0.25)
    color_gain = jnp.clip(jnp.exp(jax.random.uniform(key_list[6], (3,), jnp.float32, math.log(0.5), math.log(3.0))), 0.5, 3.0)
    color_bias = jnp.clip(jax.random.uniform(key_list[7], (3,), jnp.float32, -1.5, 1.5), -1.5, 1.5)
    return {"cells": cells, "counts": counts, "donor_dest": donor_dest, "donor_tile": donor_tile, "depth_rank": depth_rank, "resample": resample, "color_gain": color_gain, "color_bias": color_bias}


def integrate(samples, color_gain, color_bias, opacity_step):
    half_pixels = samples.shape[1]
    radiance = jnp.zeros((3, half_pixels), jnp.float32)
    transmit = jnp.ones((half_pixels,), jnp.float32)
    for layer in range(samples.shape[0]):
        sample_row = samples[layer]
        opacity = 1.0 - jnp.exp(-opacity_step * jax.nn.softplus(sample_row))
        emitted = jax.nn.sigmoid(color_gain[:, None] * sample_row[None, :] + color_bias[:, None])
        radiance = radiance + (transmit * opacity)[None, :] * emitted
        transmit = transmit * (1.0 - opacity)
    return jnp.concatenate([radiance, (1.0 - transmit)[None, :]], axis=0)


def reference(cells, counts, donor_dest, donor_tile, depth_rank, resample, color_gain, color_bias):
    owners = N_GRP * N_SWAP
    half_pixels = IMG_H // N_GRP * IMG_W
    tile_count = DEPTH * half_pixels // TS
    opacity_step = 2.5 / (DEPTH * N_SWAP)
    cell_lanes = jnp.arange(BC, dtype=jnp.int32)
    masked = jnp.where(cell_lanes[None, :] < counts[:, None], cells.astype(jnp.float32), jnp.zeros((), jnp.float32))
    segment_ids = (donor_dest[:, 0] * tile_count + donor_tile).astype(jnp.int32)
    tile_cells = jax.ops.segment_sum(masked, segment_ids, num_segments=owners * tile_count)
    tile_cells = tile_cells.astype(jnp.bfloat16).reshape(owners, tile_count, BC)
    weights = resample.astype(jnp.float32)
    inverse = jnp.argsort(depth_rank).astype(jnp.int32)

    def brick(brick_index):
        block_rows = tile_cells[brick_index].astype(jnp.float32)
        samples = jnp.dot(block_rows, weights, precision=lax.Precision.HIGHEST, preferred_element_type=jnp.float32)
        return integrate(samples.reshape(DEPTH, half_pixels), color_gain, color_bias, opacity_step)

    def advance(state_pair, rank_index):
        radiance, transmit = state_pair
        source = inverse[rank_index]
        parts = lax.map(lambda group_row: brick(group_row * N_SWAP + source), jnp.arange(N_GRP, dtype=jnp.int32))
        radiance = radiance + transmit[:, None, :] * parts[:, :3]
        transmit = transmit * (1.0 - parts[:, 3])
        return (radiance, transmit), None

    start = (jnp.zeros((N_GRP, 3, half_pixels), jnp.float32), jnp.ones((N_GRP, half_pixels), jnp.float32))
    (radiance, transmit), _ = lax.scan(advance, start, jnp.arange(N_SWAP, dtype=jnp.int32))
    frame_all = jnp.concatenate([radiance, (1.0 - transmit)[:, None, :]], axis=1)
    return jnp.transpose(frame_all, (1, 0, 2)).reshape(4, N_GRP * half_pixels)
```

```python
import functools

import jax
import jax.numpy as jnp
from jax import lax
from jax.experimental import pallas as pl
from jax.experimental.pallas import tpu as pltpu
from jax.sharding import PartitionSpec as P

IMG_W = 1024
IMG_H = 1024
DEPTH = 4
LANE_CHUNK = 256


def render_kernel(opacity_step, brick_of, gain, bias, cells_ref, resample_ref, out_ref, sample_ref):
    bricks, _, rows, width = cells_ref.shape
    sub = rows // DEPTH
    tile_span = resample_ref.shape[1]
    half_gain = [0.5 * gain[k] for k in range(3)]
    half_bias = [0.5 * bias[k] for k in range(3)]
    for chunk in range(tile_span // LANE_CHUNK):
        lanes = pl.ds(chunk * LANE_CHUNK, LANE_CHUNK)
        sample_ref[...] = jnp.dot(
            cells_ref[...].reshape(bricks * rows, width),
            resample_ref[:, lanes],
            preferred_element_type=jnp.float32,
        )

        def brick_step(place, carry):
            transmit, colors = carry[0], list(carry[1:])
            start = brick_of[place] * rows
            for layer in range(DEPTH):
                v = sample_ref[pl.ds(pl.multiple_of(start + layer * sub, sub), sub), :]
                softplus = jnp.maximum(v, 0.0) + jnp.log(1.0 + jnp.exp(-jnp.abs(v)))
                passed = transmit * jnp.exp(-opacity_step * softplus)
                weight = transmit - passed
                for k in range(3):
                    colors[k] = colors[k] + weight * jnp.tanh(half_gain[k] * v + half_bias[k])
                transmit = passed
            return (transmit, *colors)

        zero = jnp.zeros((sub, LANE_CHUNK), jnp.float32)
        done = lax.fori_loop(0, bricks, brick_step, (zero + 1.0, zero, zero, zero), unroll=4)
        opacity = 1.0 - done[0]
        for k in range(3):
            out_ref[k, :, lanes] = 0.5 * (opacity + done[1 + k])
        out_ref[3, :, lanes] = opacity


def render(cells, resample, depth_rank, color_gain, color_bias, opacity_step):
    bricks, groups, rows, width = cells.shape
    sub = rows // DEPTH
    tile_span = resample.shape[1]
    places = jnp.arange(bricks, dtype=jnp.int32)
    brick_of = jnp.sum(
        jnp.where(depth_rank[None, :] == places[:, None], places[None, :], 0), axis=1
    )
    return pl.pallas_call(
        functools.partial(render_kernel, opacity_step),
        out_shape=jax.ShapeDtypeStruct((4, groups * sub, tile_span), jnp.float32),
        grid_spec=pltpu.PrefetchScalarGridSpec(
            num_scalar_prefetch=3,
            grid=(groups,),
            in_specs=[
                pl.BlockSpec((bricks, 1, rows, width), lambda i, *_: (0, i, 0, 0)),
                pl.BlockSpec((width, tile_span), lambda i, *_: (0, 0)),
            ],
            out_specs=pl.BlockSpec((4, sub, tile_span), lambda i, *_: (0, i, 0)),
            scratch_shapes=[pltpu.VMEM((bricks * rows, LANE_CHUNK), jnp.float32)],
        ),
    )(brick_of, color_gain, color_bias, cells, resample)


def on_device(cells, counts, donor_dest, donor_tile, depth_rank, resample, color_gain, color_bias):
    owners = lax.axis_size(("grp", "swap"))
    group_count = lax.axis_size("grp")
    swap_count = lax.axis_size("swap")
    block_count, block_width = cells.shape
    tile_span = resample.shape[1]
    capacity = max(2, (3 * block_count + 2 * owners - 1) // (2 * owners))
    half_pixels = IMG_H // group_count * IMG_W
    tile_count = DEPTH * half_pixels // tile_span
    opacity_step = 2.5 / (DEPTH * swap_count)
    cell_lanes = jnp.arange(block_width, dtype=jnp.int32)
    masked = jnp.where(cell_lanes[None, :] < counts[:, None], cells, jnp.zeros_like(cells))
    target = donor_dest[:, 0]
    dest_hits = (target[:, None] == jnp.arange(owners, dtype=jnp.int32)[None, :]).astype(jnp.int32)
    before = jnp.cumsum(dest_hits, axis=0) - dest_hits
    order_in = jnp.sum(before * dest_hits, axis=1)
    slot_index = target * capacity + order_in
    layer_tiles = tile_count // DEPTH
    own_tiles = layer_tiles // swap_count
    sub = min(8, own_tiles)
    layer, place = donor_tile // layer_tiles, donor_tile % layer_tiles
    row_of = ((place // sub) * DEPTH + layer) * sub + place % sub
    send_cells = jnp.zeros((owners * capacity, block_width), cells.dtype).at[slot_index].set(masked)
    send_rows = jnp.full((owners * capacity,), -1, jnp.int32).at[slot_index].set(row_of)
    recv_cells, recv_rows = (
        lax.all_to_all(send_cells, ("grp", "swap"), split_axis=0, concat_axis=0, tiled=True),
        lax.all_to_all(send_rows, ("grp", "swap"), split_axis=0, concat_axis=0, tiled=True),
    )
    selector = (recv_rows[None, :] == jnp.arange(tile_count, dtype=jnp.int32)[:, None]).astype(
        jnp.bfloat16
    )
    tile_cells = jnp.dot(selector, recv_cells, preferred_element_type=jnp.float32).astype(
        jnp.bfloat16
    )
    bricks = lax.all_to_all(tile_cells, "swap", split_axis=0, concat_axis=0, tiled=True)
    bricks = bricks.reshape(swap_count, own_tiles // sub, DEPTH * sub, block_width)
    frame = render(bricks, resample, depth_rank, color_gain, color_bias, opacity_step)
    return frame.reshape(4, -1)


def solution(mesh):
    placed = (
        P(("grp", "swap"), None),
        P(("grp", "swap")),
        P(("grp", "swap"), None),
        P(("grp", "swap")),
        P(),
        P(),
        P(),
        P(),
    )
    return jax.shard_map(
        on_device, mesh=mesh, in_specs=placed, out_specs=P(None, ("grp", "swap")), check_vma=False
    )
```

```python
import functools

import jax
import jax.numpy as jnp
from jax import lax
from jax.experimental import pallas as pl
from jax.experimental.pallas import tpu as pltpu
from jax.sharding import PartitionSpec as P

IMG_W = 1024
IMG_H = 1024
DEPTH = 4
LANES = 128
ID_ROWS = 8
ID_BASE = 64
PACK_ROWS = 256
LANE_CHUNK = 256


def split(value, size):
    if size & (size - 1) == 0:
        return jnp.right_shift(value, size.bit_length() - 1), value & (size - 1)
    return value // size, value % size


def pack_kernel(plan, scalars, dest_ref, tile_ref, counts_ref, cells_ref, out_ref, masked_ref):
    owners, capacity, swap_count, layer_tiles, own_tiles, sub = plan
    block_count, width = cells_ref.shape
    columns = width // LANES
    first = scalars[0] * capacity
    group, brick = split(dest_ref[...], swap_count)
    layer, place = split(tile_ref[...], layer_tiles)
    owner, own = split(place, own_tiles)
    own_group, own_sub = split(own, sub)
    target = group * swap_count + owner
    row = ((own_group * swap_count + brick) * DEPTH + layer) * sub + own_sub
    row_high, row_low = split(row, ID_BASE)

    hits = lax.broadcasted_iota(jnp.int32, (owners, block_count), 0) == target
    hits = jnp.where(hits, 1.0, 0.0)
    step = min(256, block_count)
    earlier = lax.broadcasted_iota(jnp.int32, (step, step), 0) < lax.broadcasted_iota(
        jnp.int32, (step, step), 1
    )
    earlier = jnp.where(earlier, 1.0, 0.0).astype(jnp.bfloat16)
    total = jnp.zeros((owners, 1), jnp.float32)
    orders = []
    for start in range(0, block_count, step):
        part = hits[:, start : start + step]
        before = total + jnp.dot(
            part.astype(jnp.bfloat16), earlier, preferred_element_type=jnp.float32
        )
        orders.append(jnp.sum(before * part, axis=0, keepdims=True))
        total = total + jnp.sum(part, axis=1, keepdims=True)
    order = jnp.concatenate(orders, axis=1).astype(jnp.int32) - first
    present = (order >= 0) & (order < capacity)
    slot = jnp.where(present, target * capacity + order, -1)
    more = jnp.max(total) > (first + capacity).astype(jnp.float32)

    lane = jnp.where(present, order + scalars[1], -1)
    at_lane = lax.broadcasted_iota(jnp.int32, (LANES, block_count), 0) == lane
    hits = hits.astype(jnp.bfloat16)

    def spread(value):
        placed = jnp.where(at_lane, value.astype(jnp.float32), 0.0).astype(jnp.bfloat16)
        spread_out = lax.dot_general(
            hits, placed, (((1,), (1,)), ((), ())), preferred_element_type=jnp.float32
        )
        return spread_out[:, None, :]

    which = lax.broadcasted_iota(jnp.int32, (owners, ID_ROWS, LANES), 1)
    tags = jnp.where(which == 0, spread(row_high), jnp.where(which == 1, spread(row_low), 0.0))
    tags = jnp.where((which == 2) & more, 1.0, tags)
    out_ref[:, columns * capacity :, :] = tags.astype(jnp.bfloat16)

    live = jnp.transpose(jnp.broadcast_to(counts_ref[...], (LANES, block_count)))
    lanes = lax.broadcasted_iota(jnp.int32, (block_count, LANES), 1)
    for column in range(columns):
        at = pl.ds(column * LANES, LANES)
        keep = jnp.where(lanes + column * LANES < live, 1.0, 0.0).astype(jnp.bfloat16)
        masked_ref[:, at] = cells_ref[:, at] * keep

    rows = min(PACK_ROWS, owners * capacity)
    buckets = rows // capacity

    def gather_step(index, _):
        base = lax.broadcasted_iota(jnp.int32, (rows, block_count), 0) + index * rows
        pick = jnp.where(base == slot, 1.0, 0.0).astype(jnp.bfloat16)
        picked = jnp.dot(pick, masked_ref[...], preferred_element_type=jnp.float32)
        picked = picked.astype(jnp.bfloat16)
        for bucket in range(buckets):
            for column in range(columns):
                out_ref[index * buckets + bucket, column * capacity : (column + 1) * capacity, :] = (
                    picked[
                        bucket * capacity : (bucket + 1) * capacity,
                        column * LANES : (column + 1) * LANES,
                    ]
                )
        return 0

    lax.fori_loop(0, owners * capacity // rows, gather_step, 0)


def pack(plan, turn, my_index, dest, tile, counts, cells):
    owners, capacity = plan[:2]
    block_count, width = cells.shape
    shape = (owners, width // LANES * capacity + ID_ROWS, LANES)
    sources = LANES // capacity
    scalars = jnp.stack([turn, my_index % sources * capacity]).astype(jnp.int32)
    vmem = pl.BlockSpec(memory_space=pltpu.VMEM)
    return pl.pallas_call(
        functools.partial(pack_kernel, plan),
        out_shape=jax.ShapeDtypeStruct(shape, cells.dtype),
        in_specs=[pl.BlockSpec(memory_space=pltpu.SMEM)] + [vmem] * 4,
        out_specs=vmem,
        scratch_shapes=[pltpu.VMEM((block_count, width), cells.dtype)],
    )(scalars, dest, tile, counts, cells)


def integrate(sample_ref, out_ref, lanes, brick_of, gain, bias, opacity_step, bricks, rows):
    sub = rows // DEPTH
    half_gain = [0.5 * gain[k] for k in range(3)]
    half_bias = [0.5 * bias[k] for k in range(3)]

    def brick_step(place, carry):
        transmit, colors = carry[0], list(carry[1:])
        start = brick_of[place] * rows
        for layer in range(DEPTH):
            v = sample_ref[pl.ds(pl.multiple_of(start + layer * sub, sub), sub), :]
            softplus = jnp.maximum(v, 0.0) + jnp.log(1.0 + jnp.exp(-jnp.abs(v)))
            passed = transmit * jnp.exp(-opacity_step * softplus)
            weight = transmit - passed
            for k in range(3):
                colors[k] = colors[k] + weight * jnp.tanh(half_gain[k] * v + half_bias[k])
            transmit = passed
        return (transmit, *colors)

    zero = jnp.zeros((sub, sample_ref.shape[1]), jnp.float32)
    done = lax.fori_loop(0, bricks, brick_step, (zero + 1.0, zero, zero, zero), unroll=4)
    opacity = 1.0 - done[0]
    for k in range(3):
        out_ref[k, :, lanes] = 0.5 * (opacity + done[1 + k])
    out_ref[3, :, lanes] = opacity


def resample_and_integrate(read, resample_ref, out_ref, sample_ref, *scene):
    for start in range(0, resample_ref.shape[1], LANE_CHUNK):
        lanes = pl.ds(start, LANE_CHUNK)
        sample_ref[...] = jnp.dot(
            read(), resample_ref[:, lanes], preferred_element_type=jnp.float32
        )
        integrate(sample_ref, out_ref, lanes, *scene)


def render_kernel(
    opacity_step, bricks, brick_of, gain, bias, cells_ref, resample_ref, out_ref, sample_ref
):
    rows = cells_ref.shape[1] // bricks
    scene = (brick_of, gain, bias, opacity_step, bricks, rows)
    resample_and_integrate(lambda: cells_ref[0], resample_ref, out_ref, sample_ref, *scene)


def gather_render_kernel(
    opacity_step,
    bricks,
    capacity,
    brick_of,
    gain,
    bias,
    recv_ref,
    resample_ref,
    out_ref,
    data_ref,
    id_ref,
    tile_ref,
    sample_ref,
):
    owners = recv_ref.shape[0]
    width = resample_ref.shape[0]
    columns = width // LANES
    sources = LANES // capacity
    halves = id_ref.shape[0]
    group_rows = tile_ref.shape[0]

    @pl.when(pl.program_id(0) == 0)
    def _():
        tags = recv_ref[:, columns * capacity :, :].astype(jnp.float32)
        tags = jnp.sum(tags.reshape(owners // sources, sources, ID_ROWS, LANES), axis=1)
        ids = tags[:, 0, :] * ID_BASE + tags[:, 1, :]
        id_ref[...] = jnp.concatenate([ids[:halves], ids[halves:]], axis=1)
        for source in range(owners):
            part, inside = divmod(source, sources)
            start = (part % halves * 2 + part // halves) * LANES + inside * capacity
            for column in range(columns):
                data_ref[start : start + capacity, column * LANES : (column + 1) * LANES] = recv_ref[
                    source, column * capacity : (column + 1) * capacity, :
                ]

    base = lax.broadcasted_iota(jnp.int32, (group_rows, 2 * LANES), 0)
    base = (base + pl.program_id(0) * group_rows).astype(jnp.float32)
    picks = [
        jnp.where(base == id_ref[half : half + 1, :], 1.0, 0.0).astype(jnp.bfloat16)
        for half in range(halves)
    ]
    tile_ref[...] = jnp.dot(
        jnp.concatenate(picks, axis=1), data_ref[...], preferred_element_type=jnp.float32
    ).astype(jnp.bfloat16)
    scene = (brick_of, gain, bias, opacity_step, bricks, group_rows // bricks)
    resample_and_integrate(lambda: tile_ref[...], resample_ref, out_ref, sample_ref, *scene)


def render(kernel, source, source_spec, groups, group_rows, bricks, sub, scene, resample, scratch):
    width, tile_span = resample.shape
    return pl.pallas_call(
        kernel,
        out_shape=jax.ShapeDtypeStruct((4, groups * sub, tile_span), jnp.float32),
        grid_spec=pltpu.PrefetchScalarGridSpec(
            num_scalar_prefetch=3,
            grid=(groups,),
            in_specs=[source_spec, pl.BlockSpec((width, tile_span), lambda i, *_: (0, 0))],
            out_specs=pl.BlockSpec((4, sub, tile_span), lambda i, *_: (0, i, 0)),
            scratch_shapes=[*scratch, pltpu.VMEM((group_rows, LANE_CHUNK), jnp.float32)],
        ),
    )(*scene, source, resample)


def on_device(cells, counts, donor_dest, donor_tile, depth_rank, resample, color_gain, color_bias):
    both = ("grp", "swap")
    owners = lax.axis_size(both)
    group_count = lax.axis_size("grp")
    swap_count = lax.axis_size("swap")
    block_count, block_width = cells.shape
    tile_span = resample.shape[1]
    half_pixels = IMG_H // group_count * IMG_W
    layer_tiles = half_pixels // tile_span
    own_tiles = layer_tiles // swap_count
    sub = min(8, own_tiles)
    groups = own_tiles // sub
    group_rows = swap_count * DEPTH * sub
    opacity_step = 2.5 / (DEPTH * swap_count)
    mean = max(1, block_count // owners)
    capacity = min(LANES, (2 if mean >= 32 else 4) * mean)
    plan = (owners, capacity, swap_count, layer_tiles, own_tiles, sub)

    my_index = lax.axis_index(both)
    dest_row = donor_dest.reshape(1, block_count)
    tile_row = donor_tile.reshape(1, block_count)
    counts_row = counts.reshape(1, block_count)
    tag_row = block_width // LANES * capacity

    def exchange(turn):
        sent = pack(plan, turn, my_index, dest_row, tile_row, counts_row, cells)
        got = lax.all_to_all(sent, both, split_axis=0, concat_axis=0, tiled=True)
        return got, jnp.max(got[:, tag_row + 2, 0]) > 0

    def partial_sum(got):
        tags = got[:, tag_row : tag_row + 2, :].astype(jnp.float32)
        tags = jnp.sum(tags.reshape(-1, LANES // capacity, 2, LANES), axis=1)
        ids = (tags[:, 0] * ID_BASE + tags[:, 1]).reshape(1, -1)
        rows = jnp.arange(groups * group_rows, dtype=jnp.float32)[:, None]
        selector = (ids == rows).astype(jnp.bfloat16)
        data = got[:, :tag_row].reshape(owners, -1, capacity, LANES)
        data = data.transpose(0, 2, 1, 3).reshape(owners * capacity, block_width)
        return jnp.dot(selector, data, preferred_element_type=jnp.float32)

    places = jnp.arange(swap_count, dtype=jnp.int32)
    brick_of = jnp.sum(
        jnp.where(depth_rank[None, :] == places[:, None], places[None, :], 0), axis=1
    )
    scene = (brick_of, color_gain, color_bias)
    received, more = exchange(jnp.int32(0))

    def one_round():
        kernel = functools.partial(gather_render_kernel, opacity_step, swap_count, capacity)
        slots = owners * capacity
        return render(
            kernel,
            received,
            pl.BlockSpec(received.shape, lambda i, *_: (0, 0, 0)),
            groups,
            group_rows,
            swap_count,
            sub,
            scene,
            resample,
            [
                pltpu.VMEM((slots, block_width), jnp.bfloat16),
                pltpu.VMEM((slots // (2 * LANES), 2 * LANES), jnp.float32),
                pltpu.VMEM((group_rows, block_width), jnp.bfloat16),
            ],
        )

    def more_rounds():
        def next_round(state):
            turn, _, total = state
            got, again = exchange(turn)
            return turn + 1, again, total + partial_sum(got)

        start = (jnp.int32(1), more, partial_sum(received))
        total = lax.while_loop(lambda state: state[1], next_round, start)[2]
        tile_cells = total.astype(jnp.bfloat16).reshape(groups, group_rows, block_width)
        kernel = functools.partial(render_kernel, opacity_step, swap_count)
        return render(
            kernel,
            tile_cells,
            pl.BlockSpec((1, group_rows, block_width), lambda i, *_: (i, 0, 0)),
            groups,
            group_rows,
            swap_count,
            sub,
            scene,
            resample,
            [],
        )

    return lax.cond(more, more_rounds, one_round).reshape(4, -1)


def solution(mesh):
    placed = (
        P(("grp", "swap"), None),
        P(("grp", "swap")),
        P(("grp", "swap"), None),
        P(("grp", "swap")),
        P(),
        P(),
        P(),
        P(),
    )
    return jax.shard_map(
        on_device, mesh=mesh, in_specs=placed, out_specs=P(None, ("grp", "swap")), check_vma=False
    )
```

```python
import functools

import jax
import jax.numpy as jnp
from jax import lax
from jax.experimental import pallas as pl
from jax.experimental.pallas import tpu as pltpu
from jax.sharding import PartitionSpec as P

IMG_W = 1024
IMG_H = 1024
DEPTH = 4
LANES = 128
ID_ROWS = 8
ID_BASE = 64
BANDS = 2
BUCKET_STEP = 8
LANE_CHUNK = 256
LOG2_E = 1.4426950408889634


def split(value, size):
    if size & (size - 1) == 0:
        return jnp.right_shift(value, size.bit_length() - 1), value & (size - 1)
    return value // size, value % size


def one_hot(rows, columns, start, labels):
    row = (lax.broadcasted_iota(jnp.int32, (rows, columns), 0) + start).astype(jnp.int16)
    same = row == jnp.broadcast_to(labels.astype(jnp.int16), (rows, columns))
    return jnp.where(same, jnp.bfloat16(1), jnp.bfloat16(0))


def route(plan, scalars, dest_ref, tile_ref, counts_ref, cells_ref, slot_ref, tag_ref, masked_ref):
    owners, capacities, swap_count, layer_tiles, own_tiles, sub = plan
    block_count, width = cells_ref.shape
    group, brick = split(dest_ref[...], swap_count)
    layer, place = split(tile_ref[...], layer_tiles)
    owner, own = split(place, own_tiles)
    own_group, own_sub = split(own, sub)
    target = group * swap_count + owner
    row = ((own_group * swap_count + brick) * DEPTH + layer) * sub + own_sub
    parts = [part.astype(jnp.float32) for part in split(row, ID_BASE)]

    aimed = lax.broadcasted_iota(jnp.int32, (owners, block_count), 0) == target
    hits = [
        jnp.where(aimed & (counts_ref[...] > band * (width // BANDS)), 1.0, 0.0)
        for band in range(BANDS)
    ]
    hits = jnp.concatenate(hits, axis=0)
    step = min(256, block_count)
    earlier = lax.broadcasted_iota(jnp.int32, (step, step), 0) < lax.broadcasted_iota(
        jnp.int32, (step, step), 1
    )
    earlier = jnp.where(earlier, 1.0, 0.0).astype(jnp.bfloat16)
    total = jnp.zeros((BANDS * owners, 1), jnp.float32)
    before = []
    for start in range(0, block_count, step):
        part = hits[:, start : start + step]
        before.append(
            total
            + jnp.dot(part.astype(jnp.bfloat16), earlier, preferred_element_type=jnp.float32)
        )
        total = total + jnp.sum(part, axis=1, keepdims=True)
    before = jnp.concatenate(before, axis=1) * hits

    which = lax.broadcasted_iota(jnp.int32, (owners, ID_ROWS, LANES), 1)
    tags = jnp.zeros((owners, ID_ROWS, LANES), jnp.float32)
    for band, capacity in enumerate(capacities):
        rows = slice(band * owners, (band + 1) * owners)
        first = scalars[0] * capacity
        order = jnp.sum(before[rows], axis=0, keepdims=True).astype(jnp.int32) - first
        alive = counts_ref[...] > band * (width // BANDS)
        present = alive & (order >= 0) & (order < capacity)
        slot_ref[band : band + 1, :] = jnp.where(present, target * capacity + order, -1)
        lane = jnp.where(present, (order + scalars[1 + band]) & (LANES - 1), -1)
        at_lane = lax.broadcasted_iota(jnp.int32, (LANES, block_count), 0) == lane
        hit = hits[rows].astype(jnp.bfloat16)
        for index, part in enumerate(parts):
            placed = jnp.where(at_lane, part, 0.0).astype(jnp.bfloat16)
            spread = lax.dot_general(
                hit, placed, (((1,), (1,)), ((), ())), preferred_element_type=jnp.float32
            )
            tags = jnp.where(which == 2 * band + index, spread[:, None, :], tags)
        more = jnp.max(total[rows]) > (first + capacity).astype(jnp.float32)
        tags = jnp.where((which == 2 * BANDS + band) & more, 1.0, tags)
    tag_ref[...] = tags.astype(jnp.bfloat16)

    live = jnp.transpose(jnp.broadcast_to(counts_ref[...], (LANES, block_count)))
    lanes = lax.broadcasted_iota(jnp.int32, (block_count, LANES), 1)
    for start in range(0, width, LANES):
        at = pl.ds(start, LANES)
        keep = jnp.where(lanes + start < live, 1.0, 0.0).astype(jnp.bfloat16)
        masked_ref[:, at] = cells_ref[:, at] * keep


def pack_kernel(plan, scalars, dest_ref, tile_ref, counts_ref, cells_ref, out_ref, *scratch):
    slot_ref, tag_ref, masked_ref = scratch
    capacities = plan[1]
    block_count, width = cells_ref.shape
    buckets = out_ref.shape[0]
    band_width = width // BANDS
    index = pl.program_id(0)

    @pl.when(index == 0)
    def _():
        route(plan, scalars, dest_ref, tile_ref, counts_ref, cells_ref, *scratch)

    top = 0
    for band, capacity in enumerate(capacities):
        at_once = max(1, min(buckets, 512 // capacity))
        for base in range(0, buckets, at_once):
            rows = min(at_once, buckets - base) * capacity
            pick = one_hot(
                rows,
                block_count,
                (index * buckets + base) * capacity,
                slot_ref[band : band + 1, :],
            )
            picked = jnp.dot(
                pick,
                masked_ref[:, band * band_width : (band + 1) * band_width],
                preferred_element_type=jnp.float32,
            ).astype(jnp.bfloat16)
            for bucket in range(rows // capacity):
                for column in range(band_width // LANES):
                    out_ref[base + bucket, top + column * capacity : top + (column + 1) * capacity] = (
                        picked[
                            bucket * capacity : (bucket + 1) * capacity,
                            column * LANES : (column + 1) * LANES,
                        ]
                    )
        top += band_width // LANES * capacity
    out_ref[:, top:, :] = tag_ref[pl.ds(index * buckets, buckets)]


def pack(plan, turn, my_index, dest, tile, counts, cells):
    owners, capacities = plan[:2]
    block_count, width = cells.shape
    rows = width // BANDS // LANES * sum(capacities) + ID_ROWS
    buckets = min(BUCKET_STEP, owners)
    offsets = [my_index * capacity % LANES for capacity in capacities]
    scalars = jnp.stack([turn, *offsets]).astype(jnp.int32)
    row = pl.BlockSpec((1, block_count), lambda i, *_: (0, 0))
    return pl.pallas_call(
        functools.partial(pack_kernel, plan),
        out_shape=jax.ShapeDtypeStruct((owners, rows, LANES), cells.dtype),
        grid_spec=pltpu.PrefetchScalarGridSpec(
            num_scalar_prefetch=1,
            grid=(owners // buckets,),
            in_specs=[row, row, row, pl.BlockSpec((block_count, width), lambda i, *_: (0, 0))],
            out_specs=pl.BlockSpec((buckets, rows, LANES), lambda i, *_: (i, 0, 0)),
            scratch_shapes=[
                pltpu.VMEM((8, block_count), jnp.int32),
                pltpu.VMEM((owners, ID_ROWS, LANES), jnp.bfloat16),
                pltpu.VMEM((block_count, width), cells.dtype),
            ],
        ),
    )(scalars, dest, tile, counts, cells)


def integrate(sample_ref, out_ref, start, brick_of, gain, bias, opacity_step, bricks, rows):
    sub = rows // DEPTH
    chunk = sample_ref.shape[1]
    half_gain = [0.5 * gain[k] for k in range(3)]
    half_bias = [0.5 * bias[k] for k in range(3)]

    def brick_step(place, carry):
        transmit, colors = carry[0], list(carry[1:])
        top = brick_of[place] * rows
        for layer in range(DEPTH):
            v = sample_ref[pl.ds(pl.multiple_of(top + layer * sub, sub), sub), :]
            scaled = v * LOG2_E
            softplus = jnp.maximum(scaled, 0.0) + jnp.log2(1.0 + jnp.exp2(-jnp.abs(scaled)))
            passed = transmit * jnp.exp2(-opacity_step * softplus)
            weight = transmit - passed
            for k in range(3):
                colors[k] = colors[k] + weight * jnp.tanh(half_gain[k] * v + half_bias[k])
            transmit = passed
        return (transmit, *colors)

    zero = jnp.zeros((sub, chunk), jnp.float32)
    done = lax.fori_loop(0, bricks, brick_step, (zero + 1.0, zero, zero, zero), unroll=4)
    opacity = 1.0 - done[0]
    planes = [0.5 * (opacity + done[1 + k]) for k in range(3)] + [opacity]
    for k, plane in enumerate(planes):
        for row in range(sub):
            at = pl.ds(start + row * (out_ref.shape[1] // sub), chunk)
            out_ref[k : k + 1, at] = plane[row : row + 1]


def resample_and_integrate(read, resample_ref, out_ref, sample_ref, *scene):
    for start in range(0, resample_ref.shape[1], LANE_CHUNK):
        sample_ref[...] = jnp.dot(
            read(), resample_ref[:, start : start + LANE_CHUNK], preferred_element_type=jnp.float32
        )
        integrate(sample_ref, out_ref, start, *scene)


def render_kernel(
    opacity_step, bricks, brick_of, gain, bias, cells_ref, resample_ref, out_ref, sample_ref
):
    rows = cells_ref.shape[1] // bricks
    scene = (brick_of, gain, bias, opacity_step, bricks, rows)
    resample_and_integrate(lambda: cells_ref[0], resample_ref, out_ref, sample_ref, *scene)


def unpack(capacities, recv_ref, data_refs, id_refs):
    owners = recv_ref.shape[0]
    top = 0
    for capacity, data_ref in zip(capacities, data_refs):
        for column in range(data_ref.shape[1] // LANES):
            for source in range(owners):
                data_ref[
                    source * capacity : (source + 1) * capacity,
                    column * LANES : (column + 1) * LANES,
                ] = recv_ref[source, top : top + capacity, :]
            top += capacity
    tags = recv_ref[:, top:, :].astype(jnp.float32)
    lane = lax.broadcasted_iota(jnp.int32, (1, LANES), 1)
    for band, (capacity, id_ref) in enumerate(zip(capacities, id_refs)):
        ids = tags[:, 2 * band, :] * ID_BASE + tags[:, 2 * band + 1, :]
        for block in range(owners * capacity // LANES):
            low, high = block * LANES, (block + 1) * LANES
            row = jnp.zeros((1, LANES), jnp.float32)
            for source in range(low // capacity, -(-high // capacity)):
                part = ids[source : source + 1]
                if source * capacity < low:
                    part = jnp.where(lane < (source + 1) * capacity - low, part, 0.0)
                elif (source + 1) * capacity > high:
                    part = jnp.where(lane >= source * capacity - low, part, 0.0)
                row = row + part
            id_ref[0:1, low:high] = row.astype(jnp.int32)


def gather_render_kernel(
    opacity_step,
    bricks,
    capacities,
    brick_of,
    gain,
    bias,
    recv_ref,
    resample_ref,
    out_ref,
    *scratch,
):
    data_refs, id_refs = scratch[:BANDS], scratch[BANDS : 2 * BANDS]
    tile_ref, sample_ref = scratch[2 * BANDS :]
    group_rows = tile_ref.shape[0]

    @pl.when(pl.program_id(0) == 0)
    def _():
        unpack(capacities, recv_ref, data_refs, id_refs)

    band_width = data_refs[0].shape[1]
    for band, (data_ref, id_ref) in enumerate(zip(data_refs, id_refs)):
        pick = one_hot(
            group_rows, data_ref.shape[0], pl.program_id(0) * group_rows, id_ref[0:1, :]
        )
        tile_ref[:, band * band_width : (band + 1) * band_width] = jnp.dot(
            pick, data_ref[...], preferred_element_type=jnp.float32
        ).astype(jnp.bfloat16)
    scene = (brick_of, gain, bias, opacity_step, bricks, group_rows // bricks)
    resample_and_integrate(lambda: tile_ref[...], resample_ref, out_ref, sample_ref, *scene)


def render(kernel, source, source_spec, groups, group_rows, bricks, sub, scene, resample, scratch):
    width, tile_span = resample.shape
    return pl.pallas_call(
        kernel,
        out_shape=jax.ShapeDtypeStruct((4, groups * sub * tile_span), jnp.float32),
        grid_spec=pltpu.PrefetchScalarGridSpec(
            num_scalar_prefetch=3,
            grid=(groups,),
            in_specs=[source_spec, pl.BlockSpec((width, tile_span), lambda i, *_: (0, 0))],
            out_specs=pl.BlockSpec((4, sub * tile_span), lambda i, *_: (0, i)),
            scratch_shapes=[*scratch, pltpu.VMEM((group_rows, LANE_CHUNK), jnp.float32)],
        ),
    )(*scene, source, resample)


def slots_for(mean, owners, deviations):
    wanted = mean + deviations * mean**0.5
    capacity = min(LANES, max(8, int(-(-wanted // 8) * 8)))
    while owners * capacity % (2 * LANES):
        capacity += 8
    return capacity


def on_device(cells, counts, donor_dest, donor_tile, depth_rank, resample, color_gain, color_bias):
    both = ("grp", "swap")
    owners = lax.axis_size(both)
    group_count = lax.axis_size("grp")
    swap_count = lax.axis_size("swap")
    block_count, block_width = cells.shape
    tile_span = resample.shape[1]
    half_pixels = IMG_H // group_count * IMG_W
    layer_tiles = half_pixels // tile_span
    own_tiles = layer_tiles // swap_count
    sub = min(8, own_tiles)
    groups = own_tiles // sub
    group_rows = swap_count * DEPTH * sub
    opacity_step = 2.5 / (DEPTH * swap_count)
    mean = block_count / owners
    capacities = (slots_for(mean, owners, 5.5), slots_for(mean * 4 / 7, owners, 5.0))
    plan = (owners, capacities, swap_count, layer_tiles, own_tiles, sub)
    band_width = block_width // BANDS

    my_index = lax.axis_index(both)
    dest_row = donor_dest.reshape(1, block_count)
    tile_row = donor_tile.reshape(1, block_count)
    counts_row = counts.reshape(1, block_count)
    tag_row = band_width // LANES * sum(capacities)

    def exchange(turn):
        sent = pack(plan, turn, my_index, dest_row, tile_row, counts_row, cells)
        got = lax.all_to_all(sent, both, split_axis=0, concat_axis=0, tiled=True)
        flags = got[:, tag_row + 2 * BANDS : tag_row + 3 * BANDS, 0]
        return got, jnp.max(flags) > 0

    def partial_sum(got):
        rows = jnp.arange(groups * group_rows, dtype=jnp.float32)[:, None]
        tags = got[:, tag_row:, :].astype(jnp.float32)
        top, sums = 0, []
        for band, capacity in enumerate(capacities):
            ids = tags[:, 2 * band] * ID_BASE + tags[:, 2 * band + 1]
            source = jnp.arange(owners)[:, None]
            lane = (source * capacity + jnp.arange(capacity)[None, :]) % LANES
            ids = jnp.take_along_axis(ids, lane, axis=1).reshape(1, -1)
            selector = (ids == rows).astype(jnp.bfloat16)
            end = top + band_width // LANES * capacity
            data = got[:, top:end].reshape(owners, -1, capacity, LANES).transpose(0, 2, 1, 3)
            data = data.reshape(owners * capacity, band_width)
            sums.append(jnp.dot(selector, data, preferred_element_type=jnp.float32))
            top = end
        return jnp.concatenate(sums, axis=1)

    places = jnp.arange(swap_count, dtype=jnp.int32)
    brick_of = jnp.sum(
        jnp.where(depth_rank[None, :] == places[:, None], places[None, :], 0), axis=1
    )
    scene = (brick_of, color_gain, color_bias)
    received, more = exchange(jnp.int32(0))

    def one_round():
        kernel = functools.partial(gather_render_kernel, opacity_step, swap_count, capacities)
        slots = [owners * capacity for capacity in capacities]
        scratch = [pltpu.VMEM((count, band_width), jnp.bfloat16) for count in slots]
        scratch += [pltpu.VMEM((8, count), jnp.int32) for count in slots]
        scratch += [pltpu.VMEM((group_rows, block_width), jnp.bfloat16)]
        whole = pl.BlockSpec(received.shape, lambda i, *_: (0, 0, 0))
        shape = (groups, group_rows, swap_count, sub)
        return render(kernel, received, whole, *shape, scene, resample, scratch)

    def more_rounds():
        def next_round(state):
            turn, _, total = state
            got, again = exchange(turn)
            return turn + 1, again, total + partial_sum(got)

        start = (jnp.int32(1), more, partial_sum(received))
        total = lax.while_loop(lambda state: state[1], next_round, start)[2]
        tile_cells = total.astype(jnp.bfloat16).reshape(groups, group_rows, block_width)
        kernel = functools.partial(render_kernel, opacity_step, swap_count)
        group = pl.BlockSpec((1, group_rows, block_width), lambda i, *_: (i, 0, 0))
        shape = (groups, group_rows, swap_count, sub)
        return render(kernel, tile_cells, group, *shape, scene, resample, [])

    return lax.cond(more, more_rounds, one_round)


def solution(mesh):
    placed = (
        P(("grp", "swap"), None),
        P(("grp", "swap")),
        P(("grp", "swap"), None),
        P(("grp", "swap")),
        P(),
        P(),
        P(),
        P(),
    )
    return jax.shard_map(
        on_device, mesh=mesh, in_specs=placed, out_specs=P(None, ("grp", "swap")), check_vma=False
    )
```

```python
import functools

import jax
import jax.numpy as jnp
from jax import lax
from jax.experimental import pallas as pl
from jax.experimental.pallas import tpu as pltpu
from jax.sharding import PartitionSpec as P

IMG_W = 1024
IMG_H = 1024
DEPTH = 4
LANES = 128
ID_ROWS = 8
ID_BASE = 64
BANDS = 2
AXES = ("swap", "grp")
SELECT_ROWS = 1024
BUCKET_STEP = 8
LANE_CHUNK = 256
BRICK_STEP = 16
LOG2_E = 1.4426950408889634
EXP2_TOP = 126.0


def split(value, size):
    if size & (size - 1) == 0:
        return jnp.right_shift(value, size.bit_length() - 1), value & (size - 1)
    return value // size, value % size


def one_hot(rows, columns, start, labels):
    row = (lax.broadcasted_iota(jnp.int32, (rows, columns), 0) + start).astype(jnp.int16)
    same = row == jnp.broadcast_to(labels.astype(jnp.int16), (rows, columns))
    return jnp.where(same, jnp.bfloat16(1), jnp.bfloat16(0))


def route(plan, turn, dest_ref, tile_ref, counts_ref, slot_ref, tag_ref):
    owners, capacities, band_width, swap_count, layer_tiles, own_tiles, sub = plan
    block_count = dest_ref.shape[1]
    device = lax.axis_index(AXES)
    group, brick = split(dest_ref[...], swap_count)
    layer, place = split(tile_ref[...], layer_tiles)
    owner, own = split(place, own_tiles)
    own_group, own_sub = split(own, sub)
    target = owner * (owners // swap_count) + group
    row = ((own_group * swap_count + brick) * DEPTH + layer) * sub + own_sub
    parts = [part.astype(jnp.float32) for part in split(row, ID_BASE)]

    aimed = lax.broadcasted_iota(jnp.int32, (owners, block_count), 0) == target
    hits = [
        jnp.where(aimed & (counts_ref[...] > band * band_width), 1.0, 0.0)
        for band in range(BANDS)
    ]
    hits = jnp.concatenate(hits, axis=0)
    step = min(256, block_count)
    earlier = lax.broadcasted_iota(jnp.int32, (step, step), 0) < lax.broadcasted_iota(
        jnp.int32, (step, step), 1
    )
    earlier = jnp.where(earlier, 1.0, 0.0).astype(jnp.bfloat16)
    total = jnp.zeros((BANDS * owners, 1), jnp.float32)
    before = []
    for start in range(0, block_count, step):
        part = hits[:, start : start + step]
        before.append(
            total
            + jnp.dot(part.astype(jnp.bfloat16), earlier, preferred_element_type=jnp.float32)
        )
        total = total + jnp.sum(part, axis=1, keepdims=True)
    before = jnp.concatenate(before, axis=1) * hits

    which = lax.broadcasted_iota(jnp.int32, (owners, ID_ROWS, LANES), 1)
    tags = jnp.zeros((owners, ID_ROWS, LANES), jnp.float32)
    for band, capacity in enumerate(capacities):
        rows = slice(band * owners, (band + 1) * owners)
        first = turn * capacity
        order = jnp.sum(before[rows], axis=0, keepdims=True).astype(jnp.int32) - first
        alive = counts_ref[...] > band * band_width
        present = alive & (order >= 0) & (order < capacity)
        slot_ref[band : band + 1, :] = jnp.where(present, target * capacity + order, -1)
        lane = jnp.where(present, (order + device * capacity) & (LANES - 1), -1)
        at_lane = lax.broadcasted_iota(jnp.int32, (LANES, block_count), 0) == lane
        hit = hits[rows].astype(jnp.bfloat16)
        for index, part in enumerate(parts):
            placed = jnp.where(at_lane, part, 0.0).astype(jnp.bfloat16)
            spread = lax.dot_general(
                hit, placed, (((1,), (1,)), ((), ())), preferred_element_type=jnp.float32
            )
            tags = jnp.where(which == 2 * band + index, spread[:, None, :], tags)
        more = jnp.max(total[rows]) > (jnp.int32(first) + capacity).astype(jnp.float32)
        tags = jnp.where((which == 2 * BANDS + band) & more, 1.0, tags)
    tag_ref[...] = tags.astype(jnp.bfloat16)


def mask_dead(counts_ref, cells_ref):
    block_count, width = cells_ref.shape
    live = jnp.transpose(jnp.broadcast_to(counts_ref[...], (LANES, block_count)))
    lanes = lax.broadcasted_iota(jnp.int32, (block_count, LANES), 1)
    for start in range(0, width, LANES):
        at = pl.ds(start, LANES)
        keep = jnp.where(lanes + start < live, 1.0, 0.0).astype(jnp.bfloat16)
        cells_ref[:, at] = cells_ref[:, at] * keep


def pack_kernel(plan, turn_ref, dest_ref, tile_ref, counts_ref, cells_hbm, out_ref, *scratch):
    slot_ref, tag_ref, cells_ref, semaphore = scratch
    capacities, band_width = plan[1:3]
    block_count = dest_ref.shape[1]
    buckets = out_ref.shape[0]
    index = pl.program_id(0)

    @pl.when(index == 0)
    def _():
        copy = pltpu.make_async_copy(cells_hbm, cells_ref, semaphore)
        copy.start()
        route(plan, turn_ref[0], dest_ref, tile_ref, counts_ref, slot_ref, tag_ref)
        copy.wait()
        mask_dead(counts_ref, cells_ref)

    top = 0
    for band, capacity in enumerate(capacities):
        at_once = max(1, min(buckets, 512 // capacity))
        for base in range(0, buckets, at_once):
            rows = min(at_once, buckets - base) * capacity
            pick = one_hot(
                rows,
                block_count,
                (index * buckets + base) * capacity,
                slot_ref[band : band + 1, :],
            )
            picked = jnp.dot(
                pick,
                cells_ref[:, band * band_width : (band + 1) * band_width],
                preferred_element_type=jnp.float32,
            ).astype(jnp.bfloat16)
            for bucket in range(rows // capacity):
                for column in range(band_width // LANES):
                    out_ref[base + bucket, top + column * capacity : top + (column + 1) * capacity] = (
                        picked[
                            bucket * capacity : (bucket + 1) * capacity,
                            column * LANES : (column + 1) * LANES,
                        ]
                    )
        top += band_width // LANES * capacity
    out_ref[:, top:, :] = tag_ref[pl.ds(index * buckets, buckets)]


def pack(plan, turn, dest, tile, counts, cells):
    owners, capacities, band_width = plan[:3]
    block_count = cells.shape[0]
    rows = band_width // LANES * sum(capacities) + ID_ROWS
    buckets = min(BUCKET_STEP, owners)
    row = pl.BlockSpec((1, block_count), lambda i, *_: (0, 0))
    return pl.pallas_call(
        functools.partial(pack_kernel, plan),
        out_shape=jax.ShapeDtypeStruct((owners, rows, LANES), cells.dtype),
        grid_spec=pltpu.PrefetchScalarGridSpec(
            num_scalar_prefetch=1,
            grid=(owners // buckets,),
            in_specs=[row, row, row, pl.BlockSpec(memory_space=pl.ANY)],
            out_specs=pl.BlockSpec((buckets, rows, LANES), lambda i, *_: (i, 0, 0)),
            scratch_shapes=[
                pltpu.VMEM((8, block_count), jnp.int32),
                pltpu.VMEM((owners, ID_ROWS, LANES), jnp.bfloat16),
                pltpu.VMEM(cells.shape, cells.dtype),
                pltpu.SemaphoreType.DMA,
            ],
        ),
    )(jnp.full((1,), turn, jnp.int32), dest, tile, counts, cells)


def integrate_bricks(sample_ref, places, state, brick_of, gain, bias, opacity_step, rows):
    sub = rows // DEPTH
    half_gain = [0.5 * gain[k] for k in range(3)]
    half_bias = [0.5 * bias[k] for k in range(3)]
    transmit, *colors = state
    for place in places:
        top = brick_of[place] * rows
        for layer in range(DEPTH):
            v = sample_ref[pl.ds(pl.multiple_of(top + layer * sub, sub), sub), :]
            scaled = v * LOG2_E
            softplus = jnp.log2(1.0 + jnp.exp2(jnp.minimum(scaled, EXP2_TOP)))
            softplus = jnp.maximum(scaled, softplus)
            passed = transmit * jnp.exp2(-opacity_step * softplus)
            weight = transmit - passed
            for k in range(3):
                colors[k] = colors[k] + weight * jnp.tanh(half_gain[k] * v + half_bias[k])
            transmit = passed
    return (transmit, *colors)


def integrate(sample_ref, out_ref, start, scene, beside=None):
    brick_of, gain, bias, opacity_step, bricks, rows = scene
    sub = rows // DEPTH
    chunk = sample_ref.shape[1]
    at_once = min(BRICK_STEP, bricks)
    steps = bricks // at_once

    def step(index, state):
        if beside is not None:
            beside(index, steps)
        places = [index * at_once + place for place in range(at_once)]
        return integrate_bricks(sample_ref, places, state, brick_of, gain, bias, opacity_step, rows)

    zero = jnp.zeros((sub, chunk), jnp.float32)
    state = (zero + 1.0, zero, zero, zero)
    if steps == 1:
        state = step(0, state)
    else:
        state = lax.fori_loop(0, steps, step, state)
    opacity = 1.0 - state[0]
    planes = [0.5 * (opacity + state[1 + k]) for k in range(3)] + [opacity]
    for k, plane in enumerate(planes):
        for row in range(sub):
            at = pl.ds(start + row * (out_ref.shape[1] // sub), chunk)
            out_ref[k : k + 1, at] = plane[row : row + 1]


def resample_chunk(cells, rows, resample_ref, chunk, sample_ref):
    columns = resample_ref[:, chunk * LANE_CHUNK : (chunk + 1) * LANE_CHUNK]
    sample_ref[rows, :] = jnp.dot(cells, columns, preferred_element_type=jnp.float32)


def render_kernel(
    opacity_step, bricks, brick_of, gain, bias, cells_ref, resample_ref, out_ref, sample_ref
):
    group_rows = cells_ref.shape[1]
    scene = (brick_of, gain, bias, opacity_step, bricks, group_rows // bricks)
    for chunk in range(resample_ref.shape[1] // LANE_CHUNK):
        resample_chunk(cells_ref[0], slice(0, group_rows), resample_ref, chunk, sample_ref)
        integrate(sample_ref, out_ref, chunk * LANE_CHUNK, scene)


def unpack(capacities, recv_ref, data_refs, id_refs):
    owners = recv_ref.shape[0]
    top = 0
    for capacity, data_ref in zip(capacities, data_refs):
        for column in range(data_ref.shape[1] // LANES):
            for source in range(owners):
                data_ref[
                    source * capacity : (source + 1) * capacity,
                    column * LANES : (column + 1) * LANES,
                ] = recv_ref[source, top : top + capacity, :]
            top += capacity
    tags = recv_ref[:, top:, :].astype(jnp.float32)
    lane = lax.broadcasted_iota(jnp.int32, (1, LANES), 1)
    for band, (capacity, id_ref) in enumerate(zip(capacities, id_refs)):
        ids = tags[:, 2 * band, :] * ID_BASE + tags[:, 2 * band + 1, :]
        for block in range(owners * capacity // LANES):
            low, high = block * LANES, (block + 1) * LANES
            row = jnp.zeros((1, LANES), jnp.float32)
            for source in range(low // capacity, -(-high // capacity)):
                part = ids[source : source + 1]
                if source * capacity < low:
                    part = jnp.where(lane < (source + 1) * capacity - low, part, 0.0)
                elif (source + 1) * capacity > high:
                    part = jnp.where(lane >= source * capacity - low, part, 0.0)
                row = row + part
            id_ref[0:1, low:high] = row.astype(jnp.int32)


def select_rows(rows, data_refs, id_refs, tile_ref):
    for band, (data_ref, id_ref) in enumerate(zip(data_refs, id_refs)):
        slots, width = data_ref.shape
        pick = one_hot(rows.size, slots, rows.start, id_ref[0:1, :])
        tile_ref[rows, band * width : (band + 1) * width] = jnp.dot(
            pick, data_ref[...], preferred_element_type=jnp.float32
        ).astype(jnp.bfloat16)


def gather_render_kernel(
    opacity_step,
    bricks,
    capacities,
    groups,
    brick_of,
    gain,
    bias,
    recv_ref,
    resample_ref,
    out_ref,
    *scratch,
):
    data_refs, id_refs = scratch[:BANDS], scratch[BANDS : 2 * BANDS]
    tile_ref, *sample_refs = scratch[2 * BANDS :]
    chunks = resample_ref.shape[1] // LANE_CHUNK
    group_rows = sample_refs[0].shape[0]
    group = pl.program_id(0)

    def part_of(index, size):
        return pl.ds(pl.multiple_of(index * size, size), size)

    @pl.when(group == 0)
    def _():
        unpack(capacities, recv_ref, data_refs, id_refs)

        def start(index, _):
            select_rows(part_of(index, SELECT_ROWS), data_refs, id_refs, tile_ref)
            return 0

        lax.fori_loop(0, tile_ref.shape[0] // SELECT_ROWS, start, 0)

    def resample(rows, chunk):
        at = pl.ds(pl.multiple_of(group * group_rows + rows.start, rows.size), rows.size)
        resample_chunk(tile_ref[at, :], rows, resample_ref, chunk, sample_refs[chunk % 2])

    resample(pl.ds(0, group_rows), 0)
    scene = (brick_of, gain, bias, opacity_step, bricks, group_rows // bricks)
    for chunk in range(chunks):

        def beside(index, steps):
            if chunk + 1 < chunks:
                resample(part_of(index, group_rows // steps), chunk + 1)

        integrate(sample_refs[chunk % 2], out_ref, chunk * LANE_CHUNK, scene, beside)


def render(kernel, source, source_spec, groups, group_rows, bricks, sub, scene, resample, scratch):
    width, tile_span = resample.shape
    return pl.pallas_call(
        kernel,
        out_shape=jax.ShapeDtypeStruct((4, groups * sub * tile_span), jnp.float32),
        grid_spec=pltpu.PrefetchScalarGridSpec(
            num_scalar_prefetch=3,
            grid=(groups,),
            in_specs=[source_spec, pl.BlockSpec((width, tile_span), lambda i, *_: (0, 0))],
            out_specs=pl.BlockSpec((4, sub * tile_span), lambda i, *_: (0, i)),
            scratch_shapes=[*scratch, pltpu.VMEM((group_rows, LANE_CHUNK), jnp.float32)],
        ),
    )(*scene, source, resample)


def slots_for(mean, owners, deviations):
    wanted = mean + deviations * mean**0.5
    capacity = min(LANES, max(8, int(-(-wanted // 8) * 8)))
    while owners * capacity % (2 * LANES):
        capacity += 8
    return capacity


def on_device(cells, counts, donor_dest, donor_tile, depth_rank, resample, color_gain, color_bias):
    owners = lax.axis_size(AXES)
    group_count = lax.axis_size("grp")
    swap_count = lax.axis_size("swap")
    block_count, block_width = cells.shape
    tile_span = resample.shape[1]
    half_pixels = IMG_H // group_count * IMG_W
    layer_tiles = half_pixels // tile_span
    own_tiles = layer_tiles // swap_count
    sub = min(8, own_tiles)
    groups = own_tiles // sub
    group_rows = swap_count * DEPTH * sub
    opacity_step = 2.5 / (DEPTH * swap_count)
    mean = block_count / owners
    capacities = (slots_for(mean, owners, 5.5), slots_for(mean * 4 / 7, owners, 5.0))
    band_width = block_width // BANDS
    plan = (owners, capacities, band_width, swap_count, layer_tiles, own_tiles, sub)

    dest_row = donor_dest.reshape(1, block_count)
    tile_row = donor_tile.reshape(1, block_count)
    counts_row = counts.reshape(1, block_count)
    tag_row = band_width // LANES * sum(capacities)

    def exchange(turn):
        sent = pack(plan, turn, dest_row, tile_row, counts_row, cells)
        got = lax.all_to_all(sent, AXES, split_axis=0, concat_axis=0, tiled=True)
        flags = got[:, tag_row + 2 * BANDS : tag_row + 3 * BANDS, 0]
        return got, jnp.max(flags) > 0

    def partial_sum(got):
        rows = jnp.arange(groups * group_rows, dtype=jnp.float32)[:, None]
        tags = got[:, tag_row:, :].astype(jnp.float32)
        top, sums = 0, []
        for band, capacity in enumerate(capacities):
            ids = tags[:, 2 * band] * ID_BASE + tags[:, 2 * band + 1]
            source = jnp.arange(owners)[:, None]
            lane = (source * capacity + jnp.arange(capacity)[None, :]) % LANES
            ids = jnp.take_along_axis(ids, lane, axis=1).reshape(1, -1)
            selector = (ids == rows).astype(jnp.bfloat16)
            end = top + band_width // LANES * capacity
            data = got[:, top:end].reshape(owners, -1, capacity, LANES).transpose(0, 2, 1, 3)
            data = data.reshape(owners * capacity, band_width)
            sums.append(jnp.dot(selector, data, preferred_element_type=jnp.float32))
            top = end
        return jnp.concatenate(sums, axis=1)

    places = jnp.arange(swap_count, dtype=jnp.int32)
    brick_of = jnp.sum(
        jnp.where(depth_rank[None, :] == places[:, None], places[None, :], 0), axis=1
    )
    scene = (brick_of, color_gain, color_bias)
    received, more = exchange(jnp.int32(0))

    def one_round():
        kernel = functools.partial(gather_render_kernel, opacity_step, swap_count, capacities, groups)
        slots = [owners * capacity for capacity in capacities]
        scratch = [pltpu.VMEM((count, band_width), jnp.bfloat16) for count in slots]
        scratch += [pltpu.VMEM((8, count), jnp.int32) for count in slots]
        scratch += [pltpu.VMEM((groups * group_rows, block_width), jnp.bfloat16)]
        scratch += [pltpu.VMEM((group_rows, LANE_CHUNK), jnp.float32)]
        whole = pl.BlockSpec(received.shape, lambda i, *_: (0, 0, 0))
        shape = (groups, group_rows, swap_count, sub)
        return render(kernel, received, whole, *shape, scene, resample, scratch)

    def more_rounds():
        def next_round(state):
            turn, _, total = state
            got, again = exchange(turn)
            return turn + 1, again, total + partial_sum(got)

        start = (jnp.int32(1), more, partial_sum(received))
        total = lax.while_loop(lambda state: state[1], next_round, start)[2]
        tile_cells = total.astype(jnp.bfloat16).reshape(groups, group_rows, block_width)
        kernel = functools.partial(render_kernel, opacity_step, swap_count)
        group = pl.BlockSpec((1, group_rows, block_width), lambda i, *_: (i, 0, 0))
        shape = (groups, group_rows, swap_count, sub)
        return render(kernel, tile_cells, group, *shape, scene, resample, [])

    return lax.cond(more, more_rounds, one_round)


def solution(mesh):
    placed = (
        P(("grp", "swap"), None),
        P(("grp", "swap")),
        P(("grp", "swap"), None),
        P(("grp", "swap")),
        P(),
        P(),
        P(),
        P(),
    )
    return jax.shard_map(
        on_device, mesh=mesh, in_specs=placed, out_specs=P(None, ("grp", "swap")), check_vma=False
    )
```

```python
import functools

import jax
import jax.numpy as jnp
from jax import lax
from jax.experimental import pallas as pl
from jax.experimental.pallas import tpu as pltpu
from jax.sharding import PartitionSpec as P

IMG_W = 1024
IMG_H = 1024
DEPTH = 4
LANES = 128
MORE = 512.0
NO_LABEL = -4096.0
BANDS = 2
AXES = ("swap", "grp")
SELECT_ROWS = 384
STEP_ROWS = 256
BUCKET_STEP = 8
LOG2_E = 1.4426950408889634
EXP2_TOP = 126.0


def split(value, size):
    if size & (size - 1) == 0:
        return jnp.right_shift(value, size.bit_length() - 1), value & (size - 1)
    return value // size, value % size


def usable_slots(band, capacity):
    return capacity - 1 if band == BANDS - 1 else capacity


def one_hot(rows, columns, start, labels):
    row = (lax.broadcasted_iota(jnp.int32, (rows, columns), 0) + start).astype(jnp.int16)
    same = row == jnp.broadcast_to(labels.astype(jnp.int16), (rows, columns))
    return jnp.where(same, jnp.bfloat16(1), jnp.bfloat16(0))


def route(plan, turn, dest_ref, tile_ref, counts_ref, slot_ref, tag_ref):
    owners, capacities, band_width, swap_count, layer_tiles, own_tiles = plan
    block_count = dest_ref.shape[1]
    device = lax.axis_index(AXES)
    group, brick = split(dest_ref[...], swap_count)
    layer, place = split(tile_ref[...], layer_tiles)
    owner, own = split(place, own_tiles)
    target = owner * (owners // swap_count) + group
    parts = [own.astype(jnp.float32), (brick * DEPTH + layer).astype(jnp.float32)]

    aimed = lax.broadcasted_iota(jnp.int32, (owners, block_count), 0) == target
    hits = [
        jnp.where(aimed & (counts_ref[...] > band * band_width), 1.0, 0.0)
        for band in range(BANDS)
    ]
    hits = jnp.concatenate(hits, axis=0)
    step = min(256, block_count)
    earlier = lax.broadcasted_iota(jnp.int32, (step, step), 0) < lax.broadcasted_iota(
        jnp.int32, (step, step), 1
    )
    earlier = jnp.where(earlier, 1.0, 0.0).astype(jnp.bfloat16)
    total = jnp.zeros((BANDS * owners, 1), jnp.float32)
    before = []
    for start in range(0, block_count, step):
        part = hits[:, start : start + step]
        before.append(
            total
            + jnp.dot(part.astype(jnp.bfloat16), earlier, preferred_element_type=jnp.float32)
        )
        total = total + jnp.sum(part, axis=1, keepdims=True)
    before = jnp.concatenate(before, axis=1) * hits

    lanes = lax.broadcasted_iota(jnp.int32, (LANES, block_count), 0)
    lane_of = lax.broadcasted_iota(jnp.int32, (1, LANES), 1)
    for band, capacity in enumerate(capacities):
        rows = slice(band * owners, (band + 1) * owners)
        usable = usable_slots(band, capacity)
        first = turn * usable
        order = jnp.sum(before[rows], axis=0, keepdims=True).astype(jnp.int32) - first
        alive = counts_ref[...] > band * band_width
        present = alive & (order >= 0) & (order < usable)
        slot_ref[band : band + 1, :] = jnp.where(present, target * capacity + order, -1)
        placed = jnp.zeros((LANES, block_count), jnp.float32)
        for index, part in enumerate(parts):
            lane = (order + device * capacity + index * capacity) & (LANES - 1)
            placed = jnp.where(lanes == jnp.where(present, lane, -1), part, placed)
        tags = lax.dot_general(
            hits[rows].astype(jnp.bfloat16),
            placed.astype(jnp.bfloat16),
            (((1,), (1,)), ((), ())),
            preferred_element_type=jnp.float32,
        )
        more = jnp.max(total[rows]) > (jnp.int32(first) + usable).astype(jnp.float32)
        flag_lane = (device * capacity + 2 * capacity) & (LANES - 1)
        if band == BANDS - 1:
            more = more | more_before
            tags = tags + jnp.where((lane_of == flag_lane) & more, MORE, 0.0)
        more_before = more
        tag_ref[:, band * LANES : (band + 1) * LANES] = tags


def mask_dead(counts_ref, cells_ref):
    block_count, width = cells_ref.shape
    live = jnp.transpose(jnp.broadcast_to(counts_ref[...], (LANES, block_count)))
    lanes = lax.broadcasted_iota(jnp.int32, (block_count, LANES), 1)
    for start in range(0, width, LANES):
        at = pl.ds(start, LANES)
        keep = jnp.where(lanes + start < live, 1.0, 0.0).astype(jnp.bfloat16)
        cells_ref[:, at] = cells_ref[:, at] * keep


def pack_kernel(plan, turn_refs, dest_ref, tile_ref, counts_ref, cells_hbm, out_ref, *scratch):
    slot_ref, tag_ref, cells_ref, semaphore = scratch
    capacities, band_width = plan[1:3]
    block_count = dest_ref.shape[1]
    buckets = out_ref.shape[0]
    index = pl.program_id(0)

    @pl.when(index == 0)
    def _():
        copy = pltpu.make_async_copy(cells_hbm, cells_ref, semaphore)
        copy.start()
        turn = turn_refs[0][0] if turn_refs else 0
        route(plan, turn, dest_ref, tile_ref, counts_ref, slot_ref, tag_ref)
        copy.wait()
        mask_dead(counts_ref, cells_ref)

    top = 0
    for band, capacity in enumerate(capacities):
        at_once = max(1, min(buckets, 512 // capacity))
        for base in range(0, buckets, at_once):
            rows = min(at_once, buckets - base) * capacity
            pick = one_hot(
                rows,
                block_count,
                (index * buckets + base) * capacity,
                slot_ref[band : band + 1, :],
            )
            picked = jnp.dot(
                pick,
                cells_ref[:, band * band_width : (band + 1) * band_width],
                preferred_element_type=jnp.float32,
            )
            if band == BANDS - 1:
                first = pl.multiple_of(index * buckets, buckets) + base
                tags = tag_ref[pl.ds(first, rows // capacity), :]
                place = lax.broadcasted_iota(jnp.int32, (rows // capacity, capacity, 1), 1)
                tags = jnp.where(place == capacity - 1, tags[:, None, :], 0.0)
                picked = picked + tags.reshape(rows, BANDS * LANES)
            picked = picked.astype(jnp.bfloat16)
            for bucket in range(rows // capacity):
                for column in range(band_width // LANES):
                    out_ref[base + bucket, top + column * capacity : top + (column + 1) * capacity] = (
                        picked[
                            bucket * capacity : (bucket + 1) * capacity,
                            column * LANES : (column + 1) * LANES,
                        ]
                    )
        top += band_width // LANES * capacity


def pack(plan, turns, dest, tile, counts, cells):
    owners, capacities, band_width = plan[:3]
    block_count = cells.shape[0]
    rows = band_width // LANES * sum(capacities)
    buckets = min(BUCKET_STEP, owners)
    row = pl.BlockSpec((1, block_count), lambda i, *_: (0, 0))
    return pl.pallas_call(
        lambda *refs: pack_kernel(plan, refs[: len(turns)], *refs[len(turns) :]),
        out_shape=jax.ShapeDtypeStruct((owners, rows, LANES), cells.dtype),
        grid_spec=pltpu.PrefetchScalarGridSpec(
            num_scalar_prefetch=len(turns),
            grid=(owners // buckets,),
            in_specs=[row, row, row, pl.BlockSpec(memory_space=pl.ANY)],
            out_specs=pl.BlockSpec((buckets, rows, LANES), lambda i, *_: (i, 0, 0)),
            scratch_shapes=[
                pltpu.VMEM((8, block_count), jnp.int32),
                pltpu.VMEM((owners, BANDS * LANES), jnp.float32),
                pltpu.VMEM(cells.shape, cells.dtype),
                pltpu.SemaphoreType.DMA,
            ],
        ),
    )(*turns, dest, tile, counts, cells)


def integrate(sample_ref, empty_ref, out_ref, group, blocks, positions, gain, bias, opacity_step):
    tiles, span = empty_ref.shape[1], sample_ref.shape[1]
    sub = out_ref.shape[1] // span
    steps = STEP_ROWS // tiles
    half_gain = [0.5 * gain[k] for k in range(3)]
    half_bias = [0.5 * bias[k] for k in range(3)]

    def block_step(block, state):
        passing, fed, *colors = state
        for inside in range(steps):
            step = block * steps + inside
            at = pl.multiple_of(step * tiles + group * sub, sub)
            v = sample_ref[pl.ds(at, sub), :]
            empty = empty_ref[step, pl.ds(pl.multiple_of(group * sub, sub), sub), :]
            empty = jnp.concatenate([empty] * (span // LANES), axis=1)
            scaled = v * LOG2_E
            softplus = jnp.log2(1.0 + jnp.exp2(jnp.minimum(scaled, EXP2_TOP)))
            softplus = jnp.maximum(scaled, softplus)
            passed = passing * jnp.exp2(-opacity_step * softplus)
            weight = (passing - passed) * empty
            fed = fed + weight
            for k in range(3):
                colors[k] = colors[k] + weight * jnp.tanh(half_gain[k] * v + half_bias[k])
            passing = passed
        return (passing, fed, *colors)

    zero = jnp.zeros((sub, span), jnp.float32)
    passing, fed, *colors = lax.fori_loop(0, blocks, block_step, (zero + 1.0, zero) + (zero,) * 3)
    left = (positions - blocks * steps).astype(jnp.float32)
    opacity = 1.0 - passing * jnp.exp2(zero - opacity_step * left)
    rest = opacity - fed
    planes = [
        0.5 * (opacity + colors[k] + rest * jnp.tanh(zero + half_bias[k])) for k in range(3)
    ] + [opacity]
    for k, plane in enumerate(planes):
        for row in range(sub):
            out_ref[k : k + 1, row * span : (row + 1) * span] = plane[row : row + 1]


def render_kernel(
    opacity_step, positions, _, gain, bias, cells_ref, resample_ref, out_ref, sample_ref, empty_ref
):
    group = pl.program_id(0)
    tiles = empty_ref.shape[1]

    @pl.when(group == 0)
    def _():
        empty_ref[...] = jnp.ones(empty_ref.shape, jnp.float32)

        def resample(block, _):
            rows = pl.ds(pl.multiple_of(block * STEP_ROWS, STEP_ROWS), STEP_ROWS)
            sample_ref[rows, :] = jnp.dot(
                cells_ref[rows, :], resample_ref[...], preferred_element_type=jnp.float32
            )
            return 0

        lax.fori_loop(0, cells_ref.shape[0] // STEP_ROWS, resample, 0)

    blocks = jnp.int32(positions * tiles // STEP_ROWS)
    integrate(
        sample_ref, empty_ref, out_ref, group, blocks, positions, gain, bias, opacity_step
    )


def label_rows(tags, capacity):
    owners = tags.shape[0]
    lane = lax.broadcasted_iota(jnp.int32, (1, LANES), 1)
    blocks = []
    for block in range(owners * capacity // LANES):
        low, high = block * LANES, (block + 1) * LANES
        row = jnp.zeros((1, LANES), jnp.float32)
        for source in range(low // capacity, -(-high // capacity)):
            part = tags[source : source + 1]
            if source * capacity < low:
                part = jnp.where(lane < (source + 1) * capacity - low, part, 0.0)
            elif (source + 1) * capacity > high:
                part = jnp.where(lane >= source * capacity - low, part, 0.0)
            row = row + part
        blocks.append(row)
    return jnp.concatenate(blocks, axis=1)


def unpack(
    capacities, positions, tiles, mask, opacity_step, recv_ref, data_refs, id_refs, *counted
):
    empty_ref, block_ref = counted
    owners = recv_ref.shape[0]
    top = 0
    for capacity, data_ref in zip(capacities, data_refs):
        for column in range(data_ref.shape[1] // LANES):
            for source in range(owners):
                data_ref[
                    source * capacity : (source + 1) * capacity,
                    column * LANES : (column + 1) * LANES,
                ] = recv_ref[source, top : top + capacity, :]
            top += capacity
    rows, at_tile, at_position = [], [], []
    lane = lax.broadcasted_iota(jnp.int32, (owners, LANES), 1)
    source = lax.broadcasted_iota(jnp.int32, (owners, LANES), 0)
    first_label = top - (BANDS - 1) * capacities[-1] - 1
    for band, capacity in enumerate(capacities):
        tags = recv_ref[:, first_label + band * capacities[-1], :].astype(jnp.float32)
        usable = usable_slots(band, capacity)
        place = (lane - source * capacity) & (LANES - 1)
        tile = jnp.where(place < usable, tags, jnp.where(place < capacity, NO_LABEL, 0.0))
        position = pltpu.roll(tags, LANES - capacity, 1)
        position = jnp.where(place < usable, position, 0.0)
        tile, position = label_rows(tile, capacity), label_rows(position, capacity)
        rows.append(tile)
        at_tile.append(one_hot(tiles, owners * capacity, 0, tile.astype(jnp.int32)))
        at_position.append(one_hot(positions, owners * capacity, 0, position.astype(jnp.int32) ^ mask))
    hits = lax.dot_general(
        at_position[0],
        at_tile[0],
        (((1,), (1,)), ((), ())),
        preferred_element_type=jnp.float32,
    )
    is_fed = jnp.where(hits > 0.0, 1.0, 0.0)
    earlier = lax.broadcasted_iota(jnp.int32, (positions, positions), 1) < lax.broadcasted_iota(
        jnp.int32, (positions, positions), 0
    )
    earlier = jnp.where(earlier, 1.0, 0.0).astype(jnp.bfloat16)
    number = jnp.dot(earlier, is_fed.astype(jnp.bfloat16), preferred_element_type=jnp.float32)
    for band, id_ref in enumerate(id_refs):
        step = jnp.dot(
            number.astype(jnp.bfloat16), at_tile[band], preferred_element_type=jnp.float32
        )
        step = jnp.sum(step * at_position[band].astype(jnp.float32), axis=0, keepdims=True)
        id_ref[0:1, :] = (step * tiles + rows[band]).astype(jnp.int32)

    total = jnp.sum(is_fed, axis=0, keepdims=True)
    groups = block_ref.shape[0] - 1
    for index in range(groups):
        part = total[:, index * tiles // groups : (index + 1) * tiles // groups]
        block_ref[index] = -(-jnp.max(part).astype(jnp.int32) // (STEP_ROWS // tiles))
    block_ref[groups] = -(-jnp.max(total).astype(jnp.int32) // (SELECT_ROWS // tiles))

    hits = lax.dot_general(
        at_tile[0],
        at_position[0],
        (((1,), (1,)), ((), ())),
        preferred_element_type=jnp.float32,
    )
    until = lax.broadcasted_iota(jnp.int32, (positions, positions), 0) <= lax.broadcasted_iota(
        jnp.int32, (positions, positions), 1
    )
    until = jnp.where(until, 1.0, 0.0).astype(jnp.bfloat16)
    through = jnp.where(hits > 0.0, 1.0, 0.0).astype(jnp.bfloat16)
    through = jnp.dot(through, until, preferred_element_type=jnp.float32)
    step = lax.broadcasted_iota(jnp.int32, (positions, tiles, positions), 0).astype(jnp.float32)
    passed_over = jnp.where(through[None] <= step, 1.0, 0.0)
    passed_over = passed_over.reshape(positions * tiles, positions).astype(jnp.bfloat16)
    every = jnp.ones((positions, LANES), jnp.bfloat16)
    place = jnp.dot(passed_over, every, preferred_element_type=jnp.float32)
    place = place.reshape(positions, tiles, LANES)
    step = lax.broadcasted_iota(jnp.int32, (positions, tiles, LANES), 0).astype(jnp.float32)
    before = jnp.exp2(-opacity_step * (place - step))
    empty_ref[...] = jnp.where(place < positions, before, 0.0)


def gather_render_kernel(
    opacity_step,
    positions,
    capacities,
    depth_rank,
    gain,
    bias,
    recv_ref,
    resample_ref,
    out_ref,
    sample_ref,
    empty_ref,
    *scratch,
):
    data_refs, id_refs = scratch[:BANDS], scratch[BANDS : 2 * BANDS]
    tile_ref, block_ref = scratch[2 * BANDS :]
    group = pl.program_id(0)
    groups = block_ref.shape[0] - 1
    band_width = data_refs[0].shape[1]

    @pl.when(group == 0)
    def _():
        unpack(
            capacities,
            positions,
            empty_ref.shape[1],
            depth_rank[0] * DEPTH,
            opacity_step,
            recv_ref,
            data_refs,
            id_refs,
            empty_ref,
            block_ref,
        )

        def select(block, _):
            start = pl.multiple_of(block * SELECT_ROWS, SELECT_ROWS)
            for band, (data_ref, id_ref) in enumerate(zip(data_refs, id_refs)):
                pick = one_hot(SELECT_ROWS, data_ref.shape[0], start, id_ref[0:1, :])
                tile_ref[:, band * band_width : (band + 1) * band_width] = jnp.dot(
                    pick, data_ref[...], preferred_element_type=jnp.float32
                ).astype(jnp.bfloat16)

            def resample(part, _):
                near = pl.ds(pl.multiple_of(part * (SELECT_ROWS // 2), 16), SELECT_ROWS // 2)
                far = start + part * (SELECT_ROWS // 2)
                far = pl.ds(pl.multiple_of(far, 16), SELECT_ROWS // 2)
                sample_ref[far, :] = jnp.dot(
                    tile_ref[near, :], resample_ref[...], preferred_element_type=jnp.float32
                )
                return 0

            lax.fori_loop(0, 2, resample, 0)
            return 0

        lax.fori_loop(0, block_ref[groups], select, 0)

    blocks = block_ref[group]
    integrate(
        sample_ref, empty_ref, out_ref, group, blocks, positions, gain, bias, opacity_step
    )


def render(kernel, source, tiles, positions, scene, resample, scratch):
    width, tile_span = resample.shape
    sub = min(8, tiles)
    rows = -(-positions * tiles // SELECT_ROWS) * SELECT_ROWS
    whole = pl.BlockSpec(source.shape, lambda i, *_: (0,) * source.ndim)
    return pl.pallas_call(
        kernel,
        out_shape=pltpu.HBM((4, tiles * tile_span), jnp.float32),
        grid_spec=pltpu.PrefetchScalarGridSpec(
            num_scalar_prefetch=3,
            grid=(tiles // sub,),
            in_specs=[whole, pl.BlockSpec((width, tile_span), lambda i, *_: (0, 0))],
            out_specs=pl.BlockSpec((4, sub * tile_span), lambda i, *_: (0, i)),
            scratch_shapes=[
                pltpu.VMEM((rows, tile_span), jnp.float32),
                pltpu.VMEM((positions, tiles, LANES), jnp.float32),
                *scratch,
            ],
        ),
    )(*scene, source, resample)


def slots_for(mean, owners, deviations):
    wanted = mean + deviations * mean**0.5
    capacity = min(LANES // 2, max(8, int(-(-wanted // 8) * 8)))
    while owners * capacity % (2 * LANES):
        capacity += 8
    return capacity


def on_device(cells, counts, donor_dest, donor_tile, depth_rank, resample, color_gain, color_bias):
    owners = lax.axis_size(AXES)
    group_count = lax.axis_size("grp")
    swap_count = lax.axis_size("swap")
    block_count, block_width = cells.shape
    tile_span = resample.shape[1]
    half_pixels = IMG_H // group_count * IMG_W
    layer_tiles = half_pixels // tile_span
    own_tiles = layer_tiles // swap_count
    positions = swap_count * DEPTH
    opacity_step = 2.5 / (DEPTH * swap_count)
    mean = block_count / owners
    capacities = (slots_for(mean, owners, 5.5), slots_for(mean * 4 / 7, owners, 5.0))
    band_width = block_width // BANDS
    plan = (owners, capacities, band_width, swap_count, layer_tiles, own_tiles)

    dest_row = donor_dest.reshape(1, block_count)
    tile_row = donor_tile.reshape(1, block_count)
    counts_row = counts.reshape(1, block_count)
    tag_row = band_width // LANES * sum(capacities) - (BANDS - 1) * capacities[-1] - 1

    def exchange(*turns):
        sent = pack(plan, turns, dest_row, tile_row, counts_row, cells)
        got = lax.all_to_all(sent, AXES, split_axis=0, concat_axis=0, tiled=True)
        return got, jnp.max(got[:, tag_row + (BANDS - 1) * capacities[-1]]) >= MORE

    def partial_sum(got):
        rows = jnp.arange(own_tiles * positions, dtype=jnp.int32)[:, None]
        top, sums = 0, []
        for band, capacity in enumerate(capacities):
            tags = got[:, tag_row + band * capacities[-1]].astype(jnp.int32)
            source = jnp.arange(owners)[:, None]
            slot = jnp.arange(capacity)[None, :]
            lane = source * capacity + slot
            tile = jnp.take_along_axis(tags, lane % LANES, axis=1)
            position = jnp.take_along_axis(tags, (lane + capacity) % LANES, axis=1)
            ids = (position ^ (depth_rank[0] * DEPTH)) * own_tiles + tile
            ids = jnp.where(slot < usable_slots(band, capacity), ids, -1).reshape(1, -1)
            selector = (ids == rows).astype(jnp.bfloat16)
            end = top + band_width // LANES * capacity
            data = got[:, top:end].reshape(owners, -1, capacity, LANES).transpose(0, 2, 1, 3)
            data = data.reshape(owners * capacity, band_width)
            sums.append(jnp.dot(selector, data, preferred_element_type=jnp.float32))
            top = end
        return jnp.concatenate(sums, axis=1)

    scene = (depth_rank, color_gain, color_bias)
    received, more = exchange()

    def one_round():
        kernel = functools.partial(gather_render_kernel, opacity_step, positions, capacities)
        slots = [owners * capacity for capacity in capacities]
        scratch = [pltpu.VMEM((count, band_width), jnp.bfloat16) for count in slots]
        scratch += [pltpu.VMEM((8, count), jnp.int32) for count in slots]
        scratch += [pltpu.VMEM((SELECT_ROWS, block_width), jnp.bfloat16)]
        scratch += [pltpu.SMEM((own_tiles // min(8, own_tiles) + 1,), jnp.int32)]
        return render(kernel, received, own_tiles, positions, scene, resample, scratch)

    def more_rounds():
        def next_round(state):
            turn, _, total = state
            got, again = exchange(turn.reshape(1))
            return turn + 1, again, total + partial_sum(got)

        start = (jnp.int32(1), more, partial_sum(received))
        total = lax.while_loop(lambda state: state[1], next_round, start)[2]
        kernel = functools.partial(render_kernel, opacity_step, positions)
        tile_cells = total.astype(jnp.bfloat16)
        return render(kernel, tile_cells, own_tiles, positions, scene, resample, [])

    return lax.cond(more, more_rounds, one_round)


def solution(mesh):
    placed = (
        P(("grp", "swap"), None),
        P(("grp", "swap")),
        P(("grp", "swap"), None),
        P(("grp", "swap")),
        P(),
        P(),
        P(),
        P(),
    )
    return jax.shard_map(
        on_device, mesh=mesh, in_specs=placed, out_specs=P(None, ("grp", "swap")), check_vma=False
    )
```

```python
import functools

import jax
import jax.numpy as jnp
from jax import lax
from jax.experimental import pallas as pl
from jax.experimental.pallas import tpu as pltpu
from jax.sharding import PartitionSpec as P

IMG_W = 1024
IMG_H = 1024
DEPTH = 4
LANES = 128
MORE = 512.0
NO_LABEL = -4096.0
BANDS = 2
AXES = ("swap", "grp")
SELECT_ROWS = 384
STEP_ROWS = 256
INTEGRATE_LANES = 512
BUCKET_STEP = 8
LOG2_E = 1.4426950408889634
EXP2_TOP = 126.0


def split(value, size):
    if size & (size - 1) == 0:
        return jnp.right_shift(value, size.bit_length() - 1), value & (size - 1)
    return value // size, value % size


def usable_slots(band, capacity):
    return capacity - 1 if band == BANDS - 1 else capacity


def one_hot(rows, columns, start, labels):
    row = (lax.broadcasted_iota(jnp.int32, (rows, columns), 0) + start).astype(jnp.int16)
    same = row == jnp.broadcast_to(labels.astype(jnp.int16), (rows, columns))
    return jnp.where(same, jnp.bfloat16(1), jnp.bfloat16(0))


def route(plan, turn, dest_ref, tile_ref, counts_ref, slot_ref, tag_ref):
    owners, capacities, band_width, swap_count, layer_tiles, own_tiles = plan
    block_count = dest_ref.shape[1]
    device = lax.axis_index(AXES)
    group, brick = split(dest_ref[...], swap_count)
    layer, place = split(tile_ref[...], layer_tiles)
    owner, own = split(place, own_tiles)
    target = owner * (owners // swap_count) + group
    parts = [own.astype(jnp.float32), (brick * DEPTH + layer).astype(jnp.float32)]

    aimed = lax.broadcasted_iota(jnp.int32, (owners, block_count), 0) == target
    hits = [
        jnp.where(aimed & (counts_ref[...] > band * band_width), 1.0, 0.0)
        for band in range(BANDS)
    ]
    hits = jnp.concatenate(hits, axis=0)
    step = min(256, block_count)
    earlier = lax.broadcasted_iota(jnp.int32, (step, step), 0) < lax.broadcasted_iota(
        jnp.int32, (step, step), 1
    )
    earlier = jnp.where(earlier, 1.0, 0.0).astype(jnp.bfloat16)
    total = jnp.zeros((BANDS * owners, 1), jnp.float32)
    before = []
    for start in range(0, block_count, step):
        part = hits[:, start : start + step]
        before.append(
            total
            + jnp.dot(part.astype(jnp.bfloat16), earlier, preferred_element_type=jnp.float32)
        )
        total = total + jnp.sum(part, axis=1, keepdims=True)
    before = jnp.concatenate(before, axis=1) * hits

    lanes = lax.broadcasted_iota(jnp.int32, (LANES, block_count), 0).astype(jnp.int16)
    lane_of = lax.broadcasted_iota(jnp.int32, (1, LANES), 1)
    for band, capacity in enumerate(capacities):
        rows = slice(band * owners, (band + 1) * owners)
        usable = usable_slots(band, capacity)
        first = turn * usable
        order = jnp.sum(before[rows], axis=0, keepdims=True).astype(jnp.int32) - first
        alive = counts_ref[...] > band * band_width
        present = alive & (order >= 0) & (order < usable)
        slot_ref[band : band + 1, :] = jnp.where(present, target * capacity + order, -1)
        placed = jnp.zeros((LANES, block_count), jnp.bfloat16)
        for index, part in enumerate(parts):
            lane = (order + device * capacity + index * capacity) & (LANES - 1)
            lane = jnp.where(present, lane, -1).astype(jnp.int16)
            same = lanes == jnp.broadcast_to(lane, lanes.shape)
            part = jnp.broadcast_to(part.astype(jnp.bfloat16), lanes.shape)
            placed = jnp.where(same, part, placed)
        tags = lax.dot_general(
            hits[rows].astype(jnp.bfloat16),
            placed,
            (((1,), (1,)), ((), ())),
            preferred_element_type=jnp.float32,
        )
        more = jnp.max(total[rows]) > (jnp.int32(first) + usable).astype(jnp.float32)
        flag_lane = (device * capacity + 2 * capacity) & (LANES - 1)
        if band == BANDS - 1:
            more = more | more_before
            tags = tags + jnp.where((lane_of == flag_lane) & more, MORE, 0.0)
        more_before = more
        tag_ref[:, band * LANES : (band + 1) * LANES] = tags


def mask_dead(counts_ref, cells_ref):
    block_count, width = cells_ref.shape
    live = jnp.transpose(jnp.broadcast_to(counts_ref[...], (LANES, block_count)))
    live = live.astype(jnp.int16)
    lanes = lax.broadcasted_iota(jnp.int32, (block_count, LANES), 1).astype(jnp.int16)
    for start in range(0, width, LANES):
        at = pl.ds(start, LANES)
        alive = lanes + jnp.int16(start) < live
        cells_ref[:, at] = jnp.where(alive, cells_ref[:, at], jnp.bfloat16(0))


def pack_kernel(plan, turn_refs, dest_ref, tile_ref, counts_ref, cells_hbm, out_ref, *scratch):
    slot_ref, tag_ref, cells_ref, semaphore = scratch
    capacities, band_width = plan[1:3]
    block_count = dest_ref.shape[1]
    buckets = out_ref.shape[0]
    index = pl.program_id(0)

    @pl.when(index == 0)
    def _():
        copy = pltpu.make_async_copy(cells_hbm, cells_ref, semaphore)
        copy.start()
        turn = turn_refs[0][0] if turn_refs else 0
        route(plan, turn, dest_ref, tile_ref, counts_ref, slot_ref, tag_ref)
        copy.wait()
        mask_dead(counts_ref, cells_ref)

    top = 0
    for band, capacity in enumerate(capacities):
        at_once = max(1, min(buckets, 512 // capacity))
        for base in range(0, buckets, at_once):
            rows = min(at_once, buckets - base) * capacity
            pick = one_hot(
                rows,
                block_count,
                (index * buckets + base) * capacity,
                slot_ref[band : band + 1, :],
            )
            picked = jnp.dot(
                pick,
                cells_ref[:, band * band_width : (band + 1) * band_width],
                preferred_element_type=jnp.float32,
            )
            if band == BANDS - 1:
                first = pl.multiple_of(index * buckets, buckets) + base
                tags = tag_ref[pl.ds(first, rows // capacity), :]
                place = lax.broadcasted_iota(jnp.int32, (rows // capacity, capacity, 1), 1)
                tags = jnp.where(place == capacity - 1, tags[:, None, :], 0.0)
                picked = picked + tags.reshape(rows, BANDS * LANES)
            picked = picked.astype(jnp.bfloat16)
            for bucket in range(rows // capacity):
                for column in range(band_width // LANES):
                    out_ref[base + bucket, top + column * capacity : top + (column + 1) * capacity] = (
                        picked[
                            bucket * capacity : (bucket + 1) * capacity,
                            column * LANES : (column + 1) * LANES,
                        ]
                    )
        top += band_width // LANES * capacity


def pack(plan, turns, dest, tile, counts, cells):
    owners, capacities, band_width = plan[:3]
    block_count = cells.shape[0]
    rows = band_width // LANES * sum(capacities)
    buckets = min(BUCKET_STEP, owners)
    row = pl.BlockSpec((1, block_count), lambda i, *_: (0, 0))
    return pl.pallas_call(
        lambda *refs: pack_kernel(plan, refs[: len(turns)], *refs[len(turns) :]),
        out_shape=jax.ShapeDtypeStruct((owners, rows, LANES), cells.dtype),
        grid_spec=pltpu.PrefetchScalarGridSpec(
            num_scalar_prefetch=len(turns),
            grid=(owners // buckets,),
            in_specs=[row, row, row, pl.BlockSpec(memory_space=pl.ANY)],
            out_specs=pl.BlockSpec((buckets, rows, LANES), lambda i, *_: (i, 0, 0)),
            scratch_shapes=[
                pltpu.VMEM((8, block_count), jnp.int32),
                pltpu.VMEM((owners, BANDS * LANES), jnp.float32),
                pltpu.VMEM(cells.shape, cells.dtype),
                pltpu.SemaphoreType.DMA,
            ],
        ),
    )(*turns, dest, tile, counts, cells)


def integrate(sample_ref, empty_ref, out_ref, group, blocks, positions, gain, bias, opacity_step):
    tiles, span = empty_ref.shape[1], sample_ref.shape[1]
    sub = out_ref.shape[1] // span
    steps = STEP_ROWS // tiles
    half_gain = [0.5 * gain[k] for k in range(3)]
    half_bias = [0.5 * bias[k] for k in range(3)]
    left = (positions - blocks * steps).astype(jnp.float32)
    for start in range(0, span, INTEGRATE_LANES):
        lanes = slice(start, start + INTEGRATE_LANES)

        def block_step(block, state):
            passing, fed, *colors = state
            for inside in range(steps):
                step = block * steps + inside
                at = pl.multiple_of(step * tiles + group * sub, sub)
                v = sample_ref[pl.ds(at, sub), lanes]
                empty = empty_ref[step, pl.ds(pl.multiple_of(group * sub, sub), sub), :]
                empty = jnp.concatenate([empty] * (INTEGRATE_LANES // LANES), axis=1)
                scaled = v * LOG2_E
                softplus = jnp.log2(1.0 + jnp.exp2(jnp.minimum(scaled, EXP2_TOP)))
                softplus = jnp.maximum(scaled, softplus)
                passed = passing * jnp.exp2(-opacity_step * softplus)
                weight = (passing - passed) * empty
                fed = fed + weight
                for k in range(3):
                    colors[k] = colors[k] + weight * jnp.tanh(half_gain[k] * v + half_bias[k])
                passing = passed
            return (passing, fed, *colors)

        zero = jnp.zeros((sub, INTEGRATE_LANES), jnp.float32)
        state = (zero + 1.0, zero) + (zero,) * 3
        passing, fed, *colors = lax.fori_loop(0, blocks, block_step, state)
        opacity = 1.0 - passing * jnp.exp2(zero - opacity_step * left)
        rest = opacity - fed
        planes = [
            0.5 * (opacity + colors[k] + rest * jnp.tanh(zero + half_bias[k])) for k in range(3)
        ] + [opacity]
        for k, plane in enumerate(planes):
            for row in range(sub):
                at = row * span + start
                out_ref[k : k + 1, at : at + INTEGRATE_LANES] = plane[row : row + 1]


def render_kernel(
    opacity_step, positions, _, gain, bias, cells_ref, resample_ref, out_ref, sample_ref, empty_ref
):
    group = pl.program_id(0)
    tiles = empty_ref.shape[1]

    @pl.when(group == 0)
    def _():
        empty_ref[...] = jnp.ones(empty_ref.shape, jnp.float32)

        def resample(block, _):
            rows = pl.ds(pl.multiple_of(block * STEP_ROWS, STEP_ROWS), STEP_ROWS)
            sample_ref[rows, :] = jnp.dot(
                cells_ref[rows, :], resample_ref[...], preferred_element_type=jnp.float32
            )
            return 0

        lax.fori_loop(0, cells_ref.shape[0] // STEP_ROWS, resample, 0)

    blocks = jnp.int32(positions * tiles // STEP_ROWS)
    integrate(
        sample_ref, empty_ref, out_ref, group, blocks, positions, gain, bias, opacity_step
    )


def label_rows(tags, capacity):
    owners = tags.shape[0]
    lane = lax.broadcasted_iota(jnp.int32, (1, LANES), 1)
    blocks = []
    for block in range(owners * capacity // LANES):
        low, high = block * LANES, (block + 1) * LANES
        row = jnp.zeros((1, LANES), jnp.float32)
        for source in range(low // capacity, -(-high // capacity)):
            part = tags[source : source + 1]
            if source * capacity < low:
                part = jnp.where(lane < (source + 1) * capacity - low, part, 0.0)
            elif (source + 1) * capacity > high:
                part = jnp.where(lane >= source * capacity - low, part, 0.0)
            row = row + part
        blocks.append(row)
    return jnp.concatenate(blocks, axis=1)


def unpack(
    capacities, positions, tiles, mask, opacity_step, recv_ref, data_refs, id_refs, *counted
):
    empty_ref, block_ref = counted
    owners = recv_ref.shape[0]
    top = 0
    for capacity, data_ref in zip(capacities, data_refs):
        for column in range(data_ref.shape[1] // LANES):
            for source in range(owners):
                data_ref[
                    source * capacity : (source + 1) * capacity,
                    column * LANES : (column + 1) * LANES,
                ] = recv_ref[source, top : top + capacity, :]
            top += capacity
    rows, at_tile, at_position = [], [], []
    lane = lax.broadcasted_iota(jnp.int32, (owners, LANES), 1)
    source = lax.broadcasted_iota(jnp.int32, (owners, LANES), 0)
    first_label = top - (BANDS - 1) * capacities[-1] - 1
    for band, capacity in enumerate(capacities):
        tags = recv_ref[:, first_label + band * capacities[-1], :].astype(jnp.float32)
        usable = usable_slots(band, capacity)
        place = (lane - source * capacity) & (LANES - 1)
        tile = jnp.where(place < usable, tags, jnp.where(place < capacity, NO_LABEL, 0.0))
        position = pltpu.roll(tags, LANES - capacity, 1)
        position = jnp.where(place < usable, position, 0.0)
        tile, position = label_rows(tile, capacity), label_rows(position, capacity)
        rows.append(tile)
        at_tile.append(one_hot(tiles, owners * capacity, 0, tile.astype(jnp.int32)))
        at_position.append(one_hot(positions, owners * capacity, 0, position.astype(jnp.int32) ^ mask))
    hits = lax.dot_general(
        at_position[0],
        at_tile[0],
        (((1,), (1,)), ((), ())),
        preferred_element_type=jnp.float32,
    )
    is_fed = jnp.where(hits > 0.0, 1.0, 0.0)
    earlier = lax.broadcasted_iota(jnp.int32, (positions, positions), 1) < lax.broadcasted_iota(
        jnp.int32, (positions, positions), 0
    )
    earlier = jnp.where(earlier, 1.0, 0.0).astype(jnp.bfloat16)
    number = jnp.dot(earlier, is_fed.astype(jnp.bfloat16), preferred_element_type=jnp.float32)
    for band, id_ref in enumerate(id_refs):
        step = jnp.dot(
            number.astype(jnp.bfloat16), at_tile[band], preferred_element_type=jnp.float32
        )
        step = jnp.sum(step * at_position[band].astype(jnp.float32), axis=0, keepdims=True)
        id_ref[0:1, :] = (step * tiles + rows[band]).astype(jnp.int32)

    total = jnp.sum(is_fed, axis=0, keepdims=True)
    groups = block_ref.shape[0] - 1
    for index in range(groups):
        part = total[:, index * tiles // groups : (index + 1) * tiles // groups]
        block_ref[index] = -(-jnp.max(part).astype(jnp.int32) // (STEP_ROWS // tiles))
    block_ref[groups] = -(-jnp.max(total).astype(jnp.int32) // (SELECT_ROWS // tiles))

    hits = lax.dot_general(
        at_tile[0],
        at_position[0],
        (((1,), (1,)), ((), ())),
        preferred_element_type=jnp.float32,
    )
    until = lax.broadcasted_iota(jnp.int32, (positions, positions), 0) <= lax.broadcasted_iota(
        jnp.int32, (positions, positions), 1
    )
    until = jnp.where(until, 1.0, 0.0).astype(jnp.bfloat16)
    through = jnp.where(hits > 0.0, 1.0, 0.0).astype(jnp.bfloat16)
    through = jnp.dot(through, until, preferred_element_type=jnp.float32)
    step = lax.broadcasted_iota(jnp.int32, (positions, tiles, positions), 0).astype(jnp.float32)
    passed_over = jnp.where(through[None] <= step, 1.0, 0.0)
    passed_over = passed_over.reshape(positions * tiles, positions).astype(jnp.bfloat16)
    every = jnp.ones((positions, LANES), jnp.bfloat16)
    place = jnp.dot(passed_over, every, preferred_element_type=jnp.float32)
    place = place.reshape(positions, tiles, LANES)
    step = lax.broadcasted_iota(jnp.int32, (positions, tiles, LANES), 0).astype(jnp.float32)
    before = jnp.exp2(-opacity_step * (place - step))
    empty_ref[...] = jnp.where(place < positions, before, 0.0)


def gather_render_kernel(
    opacity_step,
    positions,
    capacities,
    depth_rank,
    gain,
    bias,
    recv_ref,
    resample_ref,
    out_ref,
    sample_ref,
    empty_ref,
    *scratch,
):
    data_refs, id_refs = scratch[:BANDS], scratch[BANDS : 2 * BANDS]
    tile_ref, block_ref = scratch[2 * BANDS :]
    group = pl.program_id(0)
    groups = block_ref.shape[0] - 1
    band_width = data_refs[0].shape[1]

    @pl.when(group == 0)
    def _():
        unpack(
            capacities,
            positions,
            empty_ref.shape[1],
            depth_rank[0] * DEPTH,
            opacity_step,
            recv_ref,
            data_refs,
            id_refs,
            empty_ref,
            block_ref,
        )

        def select(block, _):
            start = pl.multiple_of(block * SELECT_ROWS, SELECT_ROWS)
            for band, (data_ref, id_ref) in enumerate(zip(data_refs, id_refs)):
                pick = one_hot(SELECT_ROWS, data_ref.shape[0], start, id_ref[0:1, :])
                tile_ref[:, band * band_width : (band + 1) * band_width] = jnp.dot(
                    pick, data_ref[...], preferred_element_type=jnp.float32
                ).astype(jnp.bfloat16)

            def resample(part, _):
                near = pl.ds(pl.multiple_of(part * (SELECT_ROWS // 2), 16), SELECT_ROWS // 2)
                far = start + part * (SELECT_ROWS // 2)
                far = pl.ds(pl.multiple_of(far, 16), SELECT_ROWS // 2)
                sample_ref[far, :] = jnp.dot(
                    tile_ref[near, :], resample_ref[...], preferred_element_type=jnp.float32
                )
                return 0

            lax.fori_loop(0, 2, resample, 0)
            return 0

        lax.fori_loop(0, block_ref[groups], select, 0)

    blocks = block_ref[group]
    integrate(
        sample_ref, empty_ref, out_ref, group, blocks, positions, gain, bias, opacity_step
    )


def render(kernel, source, tiles, positions, scene, resample, scratch):
    width, tile_span = resample.shape
    sub = min(8, tiles)
    rows = -(-positions * tiles // SELECT_ROWS) * SELECT_ROWS
    whole = pl.BlockSpec(source.shape, lambda i, *_: (0,) * source.ndim)
    return pl.pallas_call(
        kernel,
        out_shape=pltpu.HBM((4, tiles * tile_span), jnp.float32),
        grid_spec=pltpu.PrefetchScalarGridSpec(
            num_scalar_prefetch=3,
            grid=(tiles // sub,),
            in_specs=[whole, pl.BlockSpec((width, tile_span), lambda i, *_: (0, 0))],
            out_specs=pl.BlockSpec((4, sub * tile_span), lambda i, *_: (0, i)),
            scratch_shapes=[
                pltpu.VMEM((rows, tile_span), jnp.float32),
                pltpu.VMEM((positions, tiles, LANES), jnp.float32),
                *scratch,
            ],
        ),
    )(*scene, source, resample)


def slots_for(mean, owners, deviations):
    wanted = mean + deviations * mean**0.5
    capacity = min(LANES // 2, max(8, int(-(-wanted // 8) * 8)))
    while owners * capacity % (2 * LANES):
        capacity += 8
    return capacity


def on_device(cells, counts, donor_dest, donor_tile, depth_rank, resample, color_gain, color_bias):
    owners = lax.axis_size(AXES)
    group_count = lax.axis_size("grp")
    swap_count = lax.axis_size("swap")
    block_count, block_width = cells.shape
    tile_span = resample.shape[1]
    half_pixels = IMG_H // group_count * IMG_W
    layer_tiles = half_pixels // tile_span
    own_tiles = layer_tiles // swap_count
    positions = swap_count * DEPTH
    opacity_step = 2.5 / (DEPTH * swap_count)
    mean = block_count / owners
    capacities = (slots_for(mean, owners, 5.5), slots_for(mean * 4 / 7, owners, 5.0))
    band_width = block_width // BANDS
    plan = (owners, capacities, band_width, swap_count, layer_tiles, own_tiles)

    dest_row = donor_dest.reshape(1, block_count)
    tile_row = donor_tile.reshape(1, block_count)
    counts_row = counts.reshape(1, block_count)
    tag_row = band_width // LANES * sum(capacities) - (BANDS - 1) * capacities[-1] - 1

    def exchange(*turns):
        sent = pack(plan, turns, dest_row, tile_row, counts_row, cells)
        got = lax.all_to_all(sent, AXES, split_axis=0, concat_axis=0, tiled=True)
        return got, jnp.max(got[:, tag_row + (BANDS - 1) * capacities[-1]]) >= MORE

    def partial_sum(got):
        rows = jnp.arange(own_tiles * positions, dtype=jnp.int32)[:, None]
        top, sums = 0, []
        for band, capacity in enumerate(capacities):
            tags = got[:, tag_row + band * capacities[-1]].astype(jnp.int32)
            source = jnp.arange(owners)[:, None]
            slot = jnp.arange(capacity)[None, :]
            lane = source * capacity + slot
            tile = jnp.take_along_axis(tags, lane % LANES, axis=1)
            position = jnp.take_along_axis(tags, (lane + capacity) % LANES, axis=1)
            ids = (position ^ (depth_rank[0] * DEPTH)) * own_tiles + tile
            ids = jnp.where(slot < usable_slots(band, capacity), ids, -1).reshape(1, -1)
            selector = (ids == rows).astype(jnp.bfloat16)
            end = top + band_width // LANES * capacity
            data = got[:, top:end].reshape(owners, -1, capacity, LANES).transpose(0, 2, 1, 3)
            data = data.reshape(owners * capacity, band_width)
            sums.append(jnp.dot(selector, data, preferred_element_type=jnp.float32))
            top = end
        return jnp.concatenate(sums, axis=1)

    scene = (depth_rank, color_gain, color_bias)
    received, more = exchange()

    def one_round():
        kernel = functools.partial(gather_render_kernel, opacity_step, positions, capacities)
        slots = [owners * capacity for capacity in capacities]
        scratch = [pltpu.VMEM((count, band_width), jnp.bfloat16) for count in slots]
        scratch += [pltpu.VMEM((8, count), jnp.int32) for count in slots]
        scratch += [pltpu.VMEM((SELECT_ROWS, block_width), jnp.bfloat16)]
        scratch += [pltpu.SMEM((own_tiles // min(8, own_tiles) + 1,), jnp.int32)]
        return render(kernel, received, own_tiles, positions, scene, resample, scratch)

    def more_rounds():
        def next_round(state):
            turn, _, total = state
            got, again = exchange(turn.reshape(1))
            return turn + 1, again, total + partial_sum(got)

        start = (jnp.int32(1), more, partial_sum(received))
        total = lax.while_loop(lambda state: state[1], next_round, start)[2]
        kernel = functools.partial(render_kernel, opacity_step, positions)
        tile_cells = total.astype(jnp.bfloat16)
        return render(kernel, tile_cells, own_tiles, positions, scene, resample, [])

    frame = one_round()
    return lax.cond(more, more_rounds, lambda: frame)


def solution(mesh):
    placed = (
        P(("grp", "swap"), None),
        P(("grp", "swap")),
        P(("grp", "swap"), None),
        P(("grp", "swap")),
        P(),
        P(),
        P(),
        P(),
    )
    return jax.shard_map(
        on_device, mesh=mesh, in_specs=placed, out_specs=P(None, ("grp", "swap")), check_vma=False
    )
```
